256 devices in a mesh: sa: 2 (over y_lo), gx: 16 (over z, core), gy: 8 (over x, y_hi).
Axes of the slice: x: 4, y: 4 (y_hi: 2, y_lo: 2; y = y_hi * 2 + y_lo), z: 8, core: 2. Of those that a mesh axis runs over, the one named last changes fastest.
Arguments:
- pred_frames: float32 [12, 32768], P(None, ('sa', 'gx', 'gy')), parts along dimension 1, may hold values from -52 to 52, as said below
- true_frames: float32 [12, 32768], P(None, ('sa', 'gx', 'gy')), parts along dimension 1, may hold values from -52 to 52, as said below
- pred_atoms: float32 [3, 57344], P(None, ('sa', 'gx', 'gy')), parts along dimension 1, may hold values from -52 to 52
- true_atoms: float32 [3, 57344], P(None, ('sa', 'gx', 'gy')), parts along dimension 1, may hold values from -52 to 52
- atom_mask: int32 [57344], P(('sa', 'gx', 'gy')), parts along dimension 0, may hold values from 0 to 1, as said below
- residue_types: int32 [4096], P(('sa', 'gx', 'gy')), parts along dimension 0, may hold values from 0 to 19
- swap_flags: int32 [4096], P(('sa', 'gx', 'gy')), parts along dimension 0, may hold values from 0 to 1
Outputs:
- frame_loss: float32 [32768], P(('sa', 'gx', 'gy')), parts along dimension 0
- atom_loss: float32 [57344], P(('sa', 'gx', 'gy')), parts along dimension 0
- total_loss: float32 [2], P('sa'), parts along dimension 0
The draws below stay inside these ranges and needn't reach their ends.
There are 2 independent parts, one for each index of `sa`. The reference program is written for one: setup_inputs(seed, part) draws one part's arguments, and reference() takes and returns one part's arrays. A program takes and returns all parts, laid end to end along the dimension named above; each array names one. Nothing has to cross between parts.
Inputs may be any that keep to these rules, and one draw needn't show every extreme that they name: `atom_mask`: atom slots 0 to 3 of every residue, its backbone atoms, are 1. `pred_frames`: rows 0 to 8 of each frame hold a rotation matrix, row-major; rows 9 to 11 its translation. `true_frames`: rows 0 to 8 of each frame hold a rotation matrix, row-major; rows 9 to 11 its translation.
All inputs are finite; a program needn't handle non-finite values.
Results may differ from the reference program's by a relative error of at most 0.0001.
Values sent between devices are 32-bit elements; how exact they have to be, the bound alone decides.
A program may use at most 64 MiB of HBM per device.

```python
import math
import jax
import jax.numpy as jnp
import numpy as np
from jax import lax

RES = 2048


def quaternion_rotation(quats):
    quats = quats / jnp.sqrt(jnp.sum(quats * quats, axis=0, keepdims=True) + 1e-12)
    real_part = quats[0]
    first_imag = quats[1]
    second_imag = quats[2]
    third_imag = quats[3]
    entries = [1.0 - 2.0 * (second_imag * second_imag + third_imag * third_imag), 2.0 * (first_imag * second_imag - real_part * third_imag), 2.0 * (first_imag * third_imag + real_part * second_imag), 2.0 * (first_imag * second_imag + real_part * third_imag), 1.0 - 2.0 * (first_imag * first_imag + third_imag * third_imag), 2.0 * (second_imag * third_imag - real_part * first_imag), 2.0 * (first_imag * third_imag - real_part * second_imag), 2.0 * (second_imag * third_imag + real_part * first_imag), 1.0 - 2.0 * (first_imag * first_imag + second_imag * second_imag)]
    return jnp.stack(entries, axis=0)


def geometry(key):
    frames_total = RES * 8
    atoms_total = RES * 14
    half_side = 8.0 + RES // 64
    streams = jax.random.split(jax.random.fold_in(key, 7771), 8)
    centers = jax.random.uniform(streams[0], (3, RES), jnp.float32, -half_side, half_side)
    spread = jnp.exp(jnp.log(8.0) * jnp.arange(RES, dtype=jnp.float32) / RES)
    spread = spread * jax.random.uniform(streams[1], (RES,), jnp.float32, 0.5, 1.5)
    true_rotation = quaternion_rotation(jax.random.normal(streams[2], (4, frames_total), jnp.float32))
    true_shift = (centers[:, :, None] + jax.random.uniform(streams[3], (3, RES, 8), jnp.float32, -2.0, 2.0)).reshape(3, frames_total)
    true_positions = (centers[:, :, None] + jax.random.uniform(streams[4], (3, RES, 14), jnp.float32, -3.0, 3.0)).reshape(3, atoms_total)
    frame_spread = jnp.repeat(spread, 8)
    atom_spread = jnp.repeat(spread, 14)
    tilt_axis = jax.random.normal(streams[5], (3, frames_total), jnp.float32)
    atom_noise = 0.5 * jax.random.uniform(streams[7], (3, atoms_total), jnp.float32, -1.0, 1.0)
    tilt = 0.02 * frame_spread[None, :] * tilt_axis
    delta = quaternion_rotation(jnp.concatenate([jnp.ones((1, frames_total), jnp.float32), 0.5 * tilt], axis=0))
    pred_rotation = jnp.einsum('akf,kbf->abf', true_rotation.reshape(3, 3, frames_total), delta.reshape(3, 3, frames_total)).reshape(9, frames_total)
    pred_shift = true_shift + 0.4 * frame_spread[None, :] * jax.random.uniform(streams[6], (3, frames_total), jnp.float32, -1.0, 1.0)
    pred_positions = true_positions + atom_spread[None, :] * atom_noise
    pred_frames = jnp.concatenate([pred_rotation, pred_shift], axis=0)
    true_frames = jnp.concatenate([true_rotation, true_shift], axis=0)
    return (pred_frames, true_frames, pred_positions, true_positions)


def draw_pred_frames(key, part):
    return geometry(key)[0]


def draw_true_frames(key, part):
    return geometry(key)[1]


def draw_pred_atoms(key, part):
    return geometry(key)[2]


def draw_true_atoms(key, part):
    return geometry(key)[3]


def draw_atom_mask(key, part):
    levels = jax.random.randint(jax.random.fold_in(key, 5113), (RES, 14), 0, 5)
    backbone = jnp.arange(14)[None, :] < 4
    return jnp.where(backbone | (levels > 0), 1, 0).astype(jnp.int32).reshape(RES * 14)


def place_ends(result, own_key, least, largest):
    longest = result.shape.index(max(result.shape))
    spots = []
    for shift in (0, 1):
        where = [jax.random.randint(jax.random.fold_in(own_key, axis), (), 0, length) for axis, length in enumerate(result.shape)]
        where[longest] = (where[longest] + shift) % result.shape[longest]
        spots.append(tuple(where))
    return result.at[spots[0]].set(least).at[spots[1]].set(largest)


def setup_inputs(seed: int = 0, part: int = 0) -> dict:
    seeds = jax.random.split(jax.random.key(seed), 8)
    part_splits = jax.random.split(jax.random.fold_in(seeds[7], part), 8)
    return {
        "pred_frames": draw_pred_frames(jax.random.fold_in(jax.random.fold_in(seeds[7], part), 71), part),
        "true_frames": draw_true_frames(jax.random.fold_in(jax.random.fold_in(seeds[7], part), 71), part),
        "pred_atoms": draw_pred_atoms(jax.random.fold_in(jax.random.fold_in(seeds[7], part), 71), part),
        "true_atoms": draw_true_atoms(jax.random.fold_in(jax.random.fold_in(seeds[7], part), 71), part),
        "atom_mask": draw_atom_mask(jax.random.fold_in(jax.random.fold_in(seeds[7], part), 71), part),
        "residue_types": place_ends(jax.random.randint(part_splits[5], (RES,), 0, 20), jax.random.fold_in(part_splits[5], 1), 0, 19).astype(jnp.int32),
        "swap_flags": place_ends(jax.random.randint(part_splits[6], (RES,), 0, 2), jax.random.fold_in(part_splits[6], 1), 0, 1).astype(jnp.int32),
    }


eps_square = 0.0001
clamp_length = 10.0

def residue_tables():
    atom_counts = np.array([5, 11, 8, 8, 6, 9, 9, 4, 10, 8, 8, 9, 8, 11, 7, 6, 7, 14, 12, 7])
    chi_counts = np.array([0, 4, 2, 2, 1, 3, 3, 0, 2, 2, 2, 4, 3, 2, 2, 1, 1, 2, 2, 1])
    atom_table = (np.arange(14)[None, :] < atom_counts[:, None]).astype(np.float32)
    slot_ids = np.arange(8)[None, :]
    frame_table = ((slot_ids == 0) | (slot_ids == 3) | (slot_ids >= 4) & (slot_ids - 3 <= chi_counts[:, None])).astype(np.float32)
    partner_table = np.tile(np.arange(14), (20, 1))
    for restype, swap_pairs in ((3, ((6, 7),)), (6, ((7, 8),)), (13, ((6, 7), (8, 9))), (18, ((6, 7), (8, 9)))):
        for first_slot, second_slot in swap_pairs:
            partner_table[restype, first_slot] = second_slot
            partner_table[restype, second_slot] = first_slot
    flip_table = np.zeros((20, 8), np.float32)
    flip_table[3, 5] = 1.0
    flip_table[13, 5] = 1.0
    flip_table[18, 5] = 1.0
    flip_table[6, 6] = 1.0
    sign_table = np.array([1, -1, -1, 1, -1, -1, 1, -1, -1, 1, 1, 1], np.float32)
    return (atom_table, frame_table, partner_table, flip_table, sign_table)

def type_onehot(residue_types):
    return residue_types[:, None] == jnp.arange(20, dtype=jnp.int32)[None, :]

def frame_terms(pred_frames, true_frames, residue_types, swap_flags):
    tables = residue_tables()
    onehot = type_onehot(residue_types).astype(jnp.float32)
    frame_table = jnp.asarray(tables[1], dtype=jnp.float32)
    flip_table = jnp.asarray(tables[3], dtype=jnp.float32)
    sign_table = jnp.asarray(tables[4], dtype=jnp.float32)
    exists = lax.optimization_barrier(jnp.sum(onehot[:, :, None] * frame_table[None], axis=1))
    flips = lax.optimization_barrier(jnp.sum(onehot[:, :, None] * flip_table[None], axis=1)) * swap_flags[:, None].astype(jnp.float32)
    residues = residue_types.shape[0]
    shaped = true_frames.reshape(12, residues, 8)
    resolved = jnp.where(flips[None] > 0.5, shaped * sign_table[:, None, None], shaped).reshape(12, residues * 8)
    rot_pred = pred_frames[:9]
    rot_true = resolved[:9]
    offsets = []
    for column in range(3):
        true_part = rot_true[column] * resolved[9] + rot_true[3 + column] * resolved[10] + rot_true[6 + column] * resolved[11]
        pred_part = rot_pred[column] * pred_frames[9] + rot_pred[3 + column] * pred_frames[10] + rot_pred[6 + column] * pred_frames[11]
        offsets.append(true_part - pred_part)
    return (rot_pred, rot_true, jnp.stack(offsets, axis=0), exists.reshape(residues * 8))

def atom_terms(true_atoms, atom_mask, residue_types, swap_flags):
    tables = residue_tables()
    onehot_int = type_onehot(residue_types).astype(jnp.int32)
    onehot = onehot_int.astype(jnp.float32)
    partner_table = jnp.asarray(tables[2], dtype=jnp.int32)
    atom_table = jnp.asarray(tables[0], dtype=jnp.float32)
    partners = lax.optimization_barrier(jnp.sum(onehot_int[:, :, None] * partner_table[None], axis=1)).astype(jnp.int32)
    own_slots = jnp.broadcast_to(jnp.arange(14, dtype=jnp.int32)[None, :], partners.shape)
    source = jnp.where(swap_flags[:, None] == 1, partners, own_slots).astype(jnp.int32)
    residues = residue_types.shape[0]
    shaped = true_atoms.reshape(3, residues, 14)
    resolved = jnp.take_along_axis(shaped, jnp.broadcast_to(source[None], shaped.shape), axis=2).reshape(3, residues * 14)
    mask_resolved = jnp.take_along_axis(atom_mask.reshape(residues, 14), source, axis=1)
    exists = lax.optimization_barrier(jnp.sum(onehot[:, :, None] * atom_table[None], axis=1))
    weight = (exists * mask_resolved.astype(jnp.float32)).reshape(residues * 14)
    return (resolved, weight)

def clamped_errors(frame_side, atom_side):
    rot_pred, rot_true, offset = frame_side
    pred_pos, true_pos = atom_side
    squares = jnp.zeros((offset.shape[1], pred_pos.shape[1]), jnp.float32)
    for column in range(3):
        error = offset[column][:, None]
        for axis_row in range(3):
            error = error + rot_pred[3 * axis_row + column][:, None] * pred_pos[axis_row][None, :]
            error = error - rot_true[3 * axis_row + column][:, None] * true_pos[axis_row][None, :]
        squares = squares + error * error
    return jnp.minimum(jnp.sqrt(squares + eps_square), clamp_length) / clamp_length

def reference(pred_frames, true_frames, pred_atoms, true_atoms, atom_mask, residue_types, swap_flags):
    rot_pred, rot_true, offset, exists = frame_terms(pred_frames, true_frames, residue_types, swap_flags)
    true_resolved, weight = atom_terms(true_atoms, atom_mask, residue_types, swap_flags)
    frames_total = exists.shape[0]
    block_rows = math.gcd(frames_total, 256)
    count_blocks = frames_total // block_rows

    def split_blocks(stacked):
        return stacked.reshape(stacked.shape[0], count_blocks, block_rows).transpose(1, 0, 2)
    blocks = (split_blocks(rot_pred), split_blocks(rot_true), split_blocks(offset), exists.reshape(count_blocks, block_rows))

    def scan_step(atom_sum, pieces):
        clamped = clamped_errors((pieces[0], pieces[1], pieces[2]), (pred_atoms, true_resolved))
        frame_sum = pieces[3] * lax.optimization_barrier(jnp.sum(clamped * weight[None, :], axis=1))
        atom_sum = atom_sum + lax.optimization_barrier(jnp.sum(clamped * pieces[3][:, None], axis=0))
        return (atom_sum, frame_sum)
    atom_sum, frame_sums = lax.scan(scan_step, jnp.zeros((pred_atoms.shape[1],), jnp.float32), blocks)
    frame_sum = frame_sums.reshape(frames_total)
    frame_count = jnp.sum(exists)
    atom_count = jnp.sum(weight)
    frame_loss = frame_sum / atom_count
    atom_loss = weight * atom_sum / frame_count
    total_loss = (jnp.sum(frame_sum) / (frame_count * atom_count)).reshape(1)
    return (frame_loss, atom_loss, total_loss)
```

```python
import functools

import jax
import jax.numpy as jnp
import numpy as np
from jax import lax
from jax.experimental import pallas as pl
from jax.experimental.pallas import tpu as pltpu
from jax.sharding import PartitionSpec as P

F32 = jnp.float32
BF16 = jnp.bfloat16
MESH = pl.DeviceIdType.MESH

RESIDUES = 16
FRAMES = 8 * RESIDUES
ATOMS = 14 * RESIDUES
KEPT = 6 * RESIDUES
COLS = 256
FB = 32
DEPTH = 32
EPS = 1e-6
ATOM_COUNTS = (5, 11, 8, 8, 6, 9, 9, 4, 10, 8, 8, 9, 8, 11, 7, 6, 7, 14, 12, 7)
CHI_COUNTS = (0, 4, 2, 2, 1, 3, 3, 0, 2, 2, 2, 4, 3, 2, 2, 1, 1, 2, 2, 1)


def tables():
    lane = np.arange(COLS)
    spread_atoms = (np.arange(128)[:, None] == lane[None] // 14) & (lane[None] < ATOMS)
    spread_frames = np.arange(128)[:, None] == np.arange(FRAMES)[None] // 8
    kept = np.arange(KEPT)
    slot = np.where(kept % 6 == 0, 0, kept % 6 + 2)
    keep = (8 * (kept // 6) + slot)[:, None] == np.arange(FRAMES)[None]
    frame_pick = np.zeros((48, 3 * 128), np.float32)
    atom_pick = np.zeros((DEPTH, 24), np.float32)
    for c in range(3):
        k = 0
        for i in range(3):
            for cc in range(3):
                if cc == c:
                    frame_pick[12, c * 128 + k] = 1.0
                atom_pick[k, 8 * i + cc] = 1.0
                k += 1
        for j, i in ((0, 0), (0, 1), (0, 2), (1, 0), (1, 1), (2, 0)):
            for b in range(3):
                frame_pick[16 * j + 3 * c + b, c * 128 + k] = 1.0
                atom_pick[k, 8 * i + 3 + b] = 1.0
                k += 1
        for j in range(3):
            frame_pick[16 * j + 9 + c, c * 128 + k] = 1.0
            atom_pick[k, 6] = 1.0
            k += 1
    return tuple(
        jnp.asarray(np.asarray(t, np.float32), BF16)
        for t in (spread_atoms, spread_frames, keep, frame_pick, atom_pick)
    )


def dot(a, b):
    return jnp.dot(a, b, preferred_element_type=F32)


def dot_nt(a, b):
    return lax.dot_general(a, b, (((1,), (1,)), ((), ())), preferred_element_type=F32)


def pieces(x, count):
    parts = []
    for _ in range(count):
        part = x.astype(BF16).astype(F32)
        parts.append(part)
        x = x - part
    return parts


def by_type(types, values):
    total = jnp.zeros(types.shape, F32)
    for k, value in enumerate(values):
        total = jnp.where(types == k, F32(value), total)
    return total


def kernel(
    nx, ny,
    pf_hbm, tf_hbm, pa_hbm, ta_hbm, mask_hbm, type_hbm, swap_hbm,
    sa_hbm, sf_hbm, keep_hbm, fpick_hbm, apick_hbm,
    floss_ref, aloss_ref, total_ref,
    pf, tf, pa, ta, mask, types, swaps, spread_a, spread_f, keep, fpick, apick,
    res, frames, atoms, lhs, rhs, acc_f,
    asend, arecv, fsums, totals,
    in_sem, fs_sem, fr_sem, as_sem, ar_sem, ps_sem, pr_sem, ss_sem, sr_sem, ts_sem, tr_sem,
):
    gx, gy = lax.axis_index("gx"), lax.axis_index("gy")

    def at_x(r):
        return {"gx": lax.rem(gx + r, nx)}

    def at_y(r):
        return {"gy": lax.rem(gy + r, ny)}

    barrier = pltpu.get_barrier_semaphore()
    for r in range(1, nx):
        pl.semaphore_signal(barrier, inc=1, device_id=at_x(r), device_id_type=MESH)
    for r in range(1, ny):
        pl.semaphore_signal(barrier, inc=1, device_id=at_y(r), device_id_type=MESH)

    loads = [
        pltpu.make_async_copy(src, dst, in_sem.at[k])
        for k, (src, dst) in enumerate(
            (
                (type_hbm, types), (swap_hbm, swaps), (sa_hbm, spread_a), (sf_hbm, spread_f),
                (pf_hbm, pf), (tf_hbm, tf), (pa_hbm, pa), (ta_hbm, ta), (mask_hbm, mask),
                (keep_hbm, keep), (fpick_hbm, fpick), (apick_hbm, apick),
            )
        )
    ]
    for load in loads:
        load.start()
    res[...] = jnp.zeros_like(res)
    atoms[0] = jnp.zeros((8, COLS), F32)
    acc_f[...] = jnp.zeros_like(acc_f)
    for load in loads:
        load.wait()

    kind, swap = types[...], swaps[...] == 1
    first = (kind == 3) | (kind == 13) | (kind == 18)
    third = (kind == 13) | (kind == 18)
    res[0:1, 0:RESIDUES] = by_type(kind, ATOM_COUNTS)
    res[1:2, 0:RESIDUES] = by_type(kind, CHI_COUNTS)
    res[2:3, 0:RESIDUES] = jnp.where(first & swap, F32(1), F32(0))
    res[3:4, 0:RESIDUES] = jnp.where((kind == 6) & swap, F32(1), F32(0))
    res[4:5, 0:RESIDUES] = jnp.where(third & swap, F32(1), F32(0))
    table = res[...].astype(BF16)
    of_atom = dot(table, spread_a[...])
    of_frame = dot(table, spread_f[...])

    lane = lax.broadcasted_iota(jnp.int32, (1, COLS), 1)
    slot = lane - 14 * ((lane * 4682) >> 16)
    swap_a, swap_b, swap_c = (of_atom[k : k + 1] > 0.5 for k in (2, 3, 4))
    upper = ((slot == 6) & swap_a) | ((slot == 7) & swap_b) | ((slot == 8) & swap_c)
    lower = ((slot == 7) & swap_a) | ((slot == 8) & swap_b) | ((slot == 9) & swap_c)
    atoms[0, 0:3, 0:ATOMS] = pa[...]
    atoms[0, 3:6, 0:ATOMS] = ta[...]
    atoms[0, 6:7, 0:ATOMS] = mask[...].astype(F32)
    raw = atoms[0]
    row = lax.broadcasted_iota(jnp.int32, (8, COLS), 0)
    renamed = jnp.where(
        upper & (row >= 3), pltpu.roll(raw, COLS - 1, 1),
        jnp.where(lower & (row >= 3), pltpu.roll(raw, 1, 1), raw),
    )
    weight = jnp.where(slot.astype(F32) < of_atom[0:1], renamed[6:7], F32(0))
    atoms[0] = renamed * jnp.where(row < 3, F32(0.1), F32(1.0)) * weight

    group = lax.broadcasted_iota(jnp.int32, (1, FRAMES), 1) & 7
    exists = jnp.where(
        (group == 0) | (group == 3) | ((group >= 4) & ((group - 3).astype(F32) <= of_frame[1:2])),
        F32(1), F32(0),
    )
    flips = ((group == 5) & (of_frame[2:3] > 0.5)) | ((group == 6) & (of_frame[3:4] > 0.5))
    sign = jnp.where(flips, F32(-1), F32(1))
    rot_p = [pf[k : k + 1] for k in range(12)]
    rot_t = [tf[k : k + 1] * sign if k % 3 and k < 9 else tf[k : k + 1] for k in range(12)]
    scale = -0.1 * exists
    for a in range(3):
        moved = rot_p[9 + a] * scale
        for b in range(3):
            turn = scale * (
                rot_p[3 * a] * rot_t[3 * b]
                + rot_p[3 * a + 1] * rot_t[3 * b + 1]
                + rot_p[3 * a + 2] * rot_t[3 * b + 2]
            )
            frames[0, 3 * a + b : 3 * a + b + 1] = turn
            moved = moved - turn * rot_t[9 + b]
        frames[0, 9 + a : 10 + a] = moved
    frames[0, 12:13] = exists
    frames[0, 13:16] = jnp.zeros((3, FRAMES), F32)

    pl.semaphore_wait(barrier, nx - 1 + ny - 1)

    def frame_copy(r):
        return pltpu.make_async_remote_copy(
            frames.at[0], frames.at[r], fs_sem.at[r], fr_sem.at[r], at_y(r), MESH
        )

    def atom_copy(r):
        return pltpu.make_async_remote_copy(
            atoms.at[0], atoms.at[r], as_sem.at[r], ar_sem.at[r], at_x(r), MESH
        )

    for r in range(1, nx):
        atom_copy(r).start()
    for r in range(1, ny):
        frame_copy(r).start()

    for s in range(ny):
        if s:
            frame_copy(s).wait_recv()
        split = jnp.concatenate(pieces(frames[s], 3), axis=0).astype(BF16)
        turned = dot_nt(keep[...], split).astype(BF16)
        side = dot(turned, fpick[...]).astype(BF16)
        for q in range(KEPT // FB):
            for c in range(3):
                lhs[s * (KEPT // FB) + q, c * FB : (c + 1) * FB] = side[
                    q * FB : (q + 1) * FB, c * 128 : c * 128 + DEPTH
                ]
    for s in range(nx):
        if s:
            atom_copy(s).wait_recv()
        split = jnp.concatenate(pieces(atoms[s], 3), axis=0).astype(BF16)
        rhs[s] = dot(apick[...], split).astype(BF16)

    def sum_copy(s):
        return pltpu.make_async_remote_copy(
            asend.at[s], arecv.at[s], ss_sem.at[s], sr_sem.at[s], at_x(nx - s), MESH
        )

    def segment(s, carry):
        block = rhs[s]
        columns = jnp.zeros((8, COLS), F32)
        for q in range(ny * KEPT // FB):
            e = dot(lhs[q], block)
            e0, e1, e2 = e[:FB], e[FB : 2 * FB], e[2 * FB :]
            y = jnp.minimum((e0 * e0 + e1 * e1) + (e2 * e2 + EPS), 1.0)
            clamped = y * lax.rsqrt(y)
            acc_f[q * FB : (q + 1) * FB] += clamped[:, :128] + clamped[:, 128:]
            columns = columns + clamped.reshape(FB // 8, 8, COLS).sum(axis=0)
        asend[s] = columns.sum(axis=0, keepdims=True)

        @pl.when(s > 0)
        def _():
            sum_copy(s).start()

        return carry

    lax.fori_loop(0, nx, segment, 0)

    row8 = lax.broadcasted_iota(jnp.int32, (8, 128), 0)
    partial = jnp.zeros((8, KEPT), F32)
    for s in range(ny):
        ones = jnp.where(row8 == s, F32(1), F32(0)).astype(BF16)
        for part in pieces(acc_f[s * KEPT : (s + 1) * KEPT], 3):
            partial = partial + dot_nt(ones, part.astype(BF16))
    wsum = jnp.zeros((1, COLS), F32)
    for s in range(nx):
        wsum = wsum + atoms[s, 6:7]
    fsums[0, 0:8, :] = jnp.zeros((8, 128), F32)
    fsums[0, 0:8, 0:KEPT] = partial
    fsums[0, 8:16, :] = jnp.broadcast_to(wsum[:, :128] + wsum[:, 128:], (8, 128))

    def part_copy(r):
        return pltpu.make_async_remote_copy(
            fsums.at[0], fsums.at[r], ps_sem.at[r], pr_sem.at[r], at_y(r), MESH
        )

    for r in range(1, ny):
        part_copy(r).start()
    fcount = jnp.zeros((1, FRAMES), F32)
    for s in range(ny):
        fcount = fcount + frames[s, 12:13]
    for r in range(1, ny):
        part_copy(r).wait_recv()
    both = fsums[0]
    own = fsums[0, 0:1]
    for r in range(1, ny):
        both = both + fsums[r]
        own = own + fsums[r, ny - r : ny - r + 1]
    atom_count = jnp.sum(both[8:9], axis=1, keepdims=True)
    totals[0, 0:1] = jnp.sum(both[0:8], axis=0, keepdims=True)
    totals[0, 1:8] = jnp.broadcast_to(fcount, (7, 128))

    def total_copy(r):
        return pltpu.make_async_remote_copy(
            totals.at[0], totals.at[r], ts_sem.at[r], tr_sem.at[r], at_x(r), MESH
        )

    for r in range(1, nx):
        total_copy(r).start()

    least_y = jnp.zeros((1, 128), F32) * own + EPS
    least = least_y * lax.rsqrt(least_y)
    columns = F32(nx * ny * COLS)
    rows = F32(nx * ny * KEPT)
    own_sum = jnp.zeros((1, FRAMES), F32)
    for part in pieces(own[:, :KEPT], 3):
        own_sum = own_sum + dot(part.astype(BF16), keep[...])
    floss_ref[...] = (
        frames[0, 12:13] * (own_sum - (columns - atom_count) * least) / atom_count
    )
    for s in range(1, nx):
        sum_copy(s).wait_recv()
    asum = asend[0]
    for s in range(1, nx):
        asum = asum + arecv[s]

    for r in range(1, nx):
        total_copy(r).wait_recv()
    both = totals[0]
    for r in range(1, nx):
        both = both + totals[r]
    frame_count = jnp.sum(both[1:2], axis=1, keepdims=True)
    numerator = jnp.sum(both[0:1], axis=1, keepdims=True)
    pairs = frame_count * atom_count
    total_ref[...] = (numerator - least * (rows * columns - pairs)) / pairs
    wide = jnp.concatenate([least, least], axis=1)
    aloss_ref[...] = (atoms[0, 6:7] * (asum - (rows - frame_count) * wide) / frame_count)[:, :ATOMS]

    for r in range(1, nx):
        atom_copy(r).wait_send()
        sum_copy(r).wait_send()
        total_copy(r).wait_send()
    for r in range(1, ny):
        frame_copy(r).wait_send()
        part_copy(r).wait_send()


def shards(nx, ny, pred_frames, true_frames, pred_atoms, true_atoms, atom_mask, residue_types, swap_flags):
    consts = tables()
    dma = pltpu.SemaphoreType.DMA
    blocks = ny * KEPT // FB
    ins = (
        pred_frames, true_frames, pred_atoms, true_atoms, atom_mask.reshape(1, ATOMS),
        residue_types.reshape(1, RESIDUES), swap_flags.reshape(1, RESIDUES), *consts,
    )
    floss, aloss, total = pl.pallas_call(
        functools.partial(kernel, nx, ny),
        out_shape=(
            jax.ShapeDtypeStruct((1, FRAMES), F32),
            jax.ShapeDtypeStruct((1, ATOMS), F32),
            jax.ShapeDtypeStruct((1, 128), F32),
        ),
        in_specs=[pl.BlockSpec(memory_space=pl.ANY)] * len(ins),
        out_specs=(pl.BlockSpec(memory_space=pltpu.VMEM),) * 3,
        scratch_shapes=[pltpu.VMEM(a.shape, a.dtype) for a in ins]
        + [
            pltpu.VMEM((8, 128), F32),
            pltpu.VMEM((ny, 16, FRAMES), F32),
            pltpu.VMEM((nx, 8, COLS), F32),
            pltpu.VMEM((blocks, 3 * FB, DEPTH), BF16),
            pltpu.VMEM((nx, DEPTH, COLS), BF16),
            pltpu.VMEM((ny * KEPT, 128), F32),
            pltpu.VMEM((nx, 1, COLS), F32),
            pltpu.VMEM((nx, 1, COLS), F32),
            pltpu.VMEM((ny, 16, 128), F32),
            pltpu.VMEM((nx, 8, 128), F32),
            dma((len(ins),)),
            dma((ny,)), dma((ny,)), dma((nx,)), dma((nx,)),
            dma((ny,)), dma((ny,)), dma((nx,)), dma((nx,)), dma((nx,)), dma((nx,)),
        ],
        compiler_params=pltpu.CompilerParams(collective_id=0, has_side_effects=True),
        name="fape",
    )(*ins)
    return floss.reshape(FRAMES), aloss.reshape(ATOMS), total[0, :1]


def solution(mesh):
    whole = ("sa", "gx", "gy")
    wide, flat = P(None, whole), P(whole)
    return jax.shard_map(
        functools.partial(shards, mesh.shape["gx"], mesh.shape["gy"]),
        mesh=mesh,
        in_specs=(wide, wide, wide, wide, flat, flat, flat),
        out_specs=(flat, flat, P("sa")),
        check_vma=False,
    )
```

```python
import functools

import jax
import jax.numpy as jnp
import numpy as np
from jax import lax
from jax.experimental import pallas as pl
from jax.experimental.pallas import tpu as pltpu
from jax.sharding import PartitionSpec as P

F32 = jnp.float32
BF16 = jnp.bfloat16
MESH = pl.DeviceIdType.MESH

RESIDUES = 16
FRAMES = 8 * RESIDUES
ATOMS = 14 * RESIDUES
KEPT = 6 * RESIDUES
COLS = 256
FB = 32
DEPTH = 32
EPS = 1e-6
ATOM_COUNTS = (5, 11, 8, 8, 6, 9, 9, 4, 10, 8, 8, 9, 8, 11, 7, 6, 7, 14, 12, 7)
CHI_COUNTS = (0, 4, 2, 2, 1, 3, 3, 0, 2, 2, 2, 4, 3, 2, 2, 1, 1, 2, 2, 1)


def tables():
    spread = np.zeros((RESIDUES, 384), np.float32)
    for k in range(ATOMS):
        spread[k // 14, k] = 1.0
    for k in range(FRAMES):
        spread[k // 8, COLS + k] = 1.0
    keep = np.zeros((KEPT, 384), np.float32)
    for k in range(KEPT):
        keep[k, 8 * (k // 6) + (k % 6 + 2 if k % 6 else 0)] = 1.0
    frame_pick = np.zeros((48, 384), np.float32)
    atom_pick = np.zeros((DEPTH, 384), np.float32)
    for c in range(3):
        k = 0
        for i in range(3):
            for cc in range(3):
                if cc == c:
                    frame_pick[12, c * 128 + k] = 1.0
                atom_pick[k, 8 * i + cc] = 1.0
                k += 1
        for j, i in ((0, 0), (0, 1), (0, 2), (1, 0), (1, 1), (2, 0)):
            for b in range(3):
                frame_pick[16 * j + 3 * c + b, c * 128 + k] = 1.0
                atom_pick[k, 8 * i + 3 + b] = 1.0
                k += 1
        for j in range(3):
            frame_pick[16 * j + 9 + c, c * 128 + k] = 1.0
            atom_pick[k, 6] = 1.0
            k += 1
    return jnp.asarray(np.concatenate([spread, keep, frame_pick, atom_pick]), BF16)


def dot(a, b):
    return jnp.dot(a, b, preferred_element_type=F32)


def dot_nt(a, b):
    return lax.dot_general(a, b, (((1,), (1,)), ((), ())), preferred_element_type=F32)


def pieces(x, count):
    parts = []
    for _ in range(count):
        part = x.astype(BF16).astype(F32)
        parts.append(part)
        x = x - part
    return parts


def by_type(types, values):
    total = jnp.zeros(types.shape, F32)
    for k, value in enumerate(values):
        total = jnp.where(types == k, F32(value), total)
    return total


def all_of(ref, sem):
    pltpu.make_async_copy(ref, ref, sem).wait()


def kernel(
    nx, ny,
    pf_hbm, tf_hbm, pa_hbm, ta_hbm, mask_hbm, type_hbm, swap_hbm, consts_hbm,
    out_ref,
    pf, tf, pa, ta, mask, types, swaps, consts,
    res, frames, atoms, lhs, rhs, acc_f, acc_c,
    asend, arecv, psend, precv, tsend, usend,
    in_sem, send_sem, frame_sem, atom_sem, sum_sem, part_sem, total_sems,
):
    gx, gy = lax.axis_index("gx"), lax.axis_index("gy")
    nz, nw = nx // 2, ny // 2
    z, core, w, half = lax.div(gx, 2), lax.rem(gx, 2), lax.div(gy, 2), lax.rem(gy, 2)
    near_z = [0] + [d for k in range(1, nz // 2 + 1) for d in sorted({k, nz - k})]
    near_w = [0] + [d for k in range(1, nw // 2 + 1) for d in sorted({k, nw - k})]

    def to_x(j):
        return {"gx": 2 * lax.rem(z + near_z[j // 2], nz) + lax.rem(core + j % 2, 2)}

    def from_x(j):
        return {"gx": 2 * lax.rem(z + nz - near_z[j // 2], nz) + lax.rem(core + j % 2, 2)}

    def to_y(j):
        return {"gy": 2 * lax.rem(w + near_w[j % nw], nw) + lax.rem(half + j // nw, 2)}

    def from_y(j):
        return {"gy": 2 * lax.rem(w + nw - near_w[j % nw], nw) + lax.rem(half + j // nw, 2)}

    barrier = pltpu.get_barrier_semaphore()
    for j in range(1, nx):
        pl.semaphore_signal(barrier, inc=1, device_id=to_x(j), device_id_type=MESH)
    for j in range(1, ny):
        pl.semaphore_signal(barrier, inc=1, device_id=to_y(j), device_id_type=MESH)

    loads = [
        pltpu.make_async_copy(src, dst, in_sem.at[k])
        for k, (src, dst) in enumerate(
            (
                (type_hbm, types), (swap_hbm, swaps), (consts_hbm, consts), (pf_hbm, pf),
                (tf_hbm, tf), (pa_hbm, pa), (ta_hbm, ta), (mask_hbm, mask),
            )
        )
    ]
    for load in loads:
        load.start()
    res[...] = jnp.zeros_like(res)
    atoms[0] = jnp.zeros((8, COLS), F32)
    acc_f[...] = jnp.zeros_like(acc_f)
    for load in loads:
        load.wait()
    spread = consts[0:RESIDUES]
    keep = consts[RESIDUES : RESIDUES + KEPT, 0:128]
    fpick = consts[RESIDUES + KEPT : RESIDUES + KEPT + 48]
    apick = consts[RESIDUES + KEPT + 48 : RESIDUES + KEPT + 48 + DEPTH, 0:24]

    kind, swap = types[...], swaps[...] == 1
    first = (kind == 3) | (kind == 13) | (kind == 18)
    third = (kind == 13) | (kind == 18)
    res[0:1, 0:RESIDUES] = by_type(kind, ATOM_COUNTS)
    res[1:2, 0:RESIDUES] = by_type(kind, CHI_COUNTS)
    res[2:3, 0:RESIDUES] = jnp.where(first & swap, F32(1), F32(0))
    res[3:4, 0:RESIDUES] = jnp.where((kind == 6) & swap, F32(1), F32(0))
    res[4:5, 0:RESIDUES] = jnp.where(third & swap, F32(1), F32(0))
    of_both = dot(res[:, 0:RESIDUES].astype(BF16), spread)
    of_atom, of_frame = of_both[:, :COLS], of_both[:, COLS:]

    lane = lax.broadcasted_iota(jnp.int32, (1, COLS), 1)
    slot = lane - 14 * ((lane * 4682) >> 16)
    swap_a, swap_b, swap_c = (of_atom[k : k + 1] > 0.5 for k in (2, 3, 4))
    upper = ((slot == 6) & swap_a) | ((slot == 7) & swap_b) | ((slot == 8) & swap_c)
    lower = ((slot == 7) & swap_a) | ((slot == 8) & swap_b) | ((slot == 9) & swap_c)
    atoms[0, 0:3, 0:ATOMS] = pa[...]
    atoms[0, 3:6, 0:ATOMS] = ta[...]
    atoms[0, 6:7, 0:ATOMS] = mask[...].astype(F32)
    raw = atoms[0]
    row = lax.broadcasted_iota(jnp.int32, (8, COLS), 0)
    renamed = jnp.where(
        upper & (row >= 3), pltpu.roll(raw, COLS - 1, 1),
        jnp.where(lower & (row >= 3), pltpu.roll(raw, 1, 1), raw),
    )
    weight = jnp.where(slot.astype(F32) < of_atom[0:1], renamed[6:7], F32(0))
    atoms[0] = renamed * jnp.where(row < 3, F32(0.1), F32(1.0)) * weight

    group = lax.broadcasted_iota(jnp.int32, (1, FRAMES), 1) & 7
    exists = jnp.where(
        (group == 0) | (group == 3) | ((group >= 4) & ((group - 3).astype(F32) <= of_frame[1:2])),
        F32(1), F32(0),
    )
    flips = ((group == 5) & (of_frame[2:3] > 0.5)) | ((group == 6) & (of_frame[3:4] > 0.5))
    sign = jnp.where(flips, F32(-1), F32(1))
    rot_p = [pf[k : k + 1] for k in range(12)]
    rot_t = [tf[k : k + 1] * sign if k % 3 and k < 9 else tf[k : k + 1] for k in range(12)]
    scale = -0.1 * exists
    for a in range(3):
        moved = rot_p[9 + a] * scale
        for b in range(3):
            turn = scale * (
                rot_p[3 * a] * rot_t[3 * b]
                + rot_p[3 * a + 1] * rot_t[3 * b + 1]
                + rot_p[3 * a + 2] * rot_t[3 * b + 2]
            )
            frames[0, 3 * a + b : 3 * a + b + 1] = turn
            moved = moved - turn * rot_t[9 + b]
        frames[0, 9 + a : 10 + a] = moved
    frames[0, 12:13] = exists
    frames[0, 13:16] = jnp.zeros((3, FRAMES), F32)

    pl.semaphore_wait(barrier, nx - 1 + ny - 1)

    first_part = 6 if nx >= 16 else 2
    middle = (first_part + nx) // 2
    groups = ((0, first_part), (first_part, middle), (middle, nx))
    group_of = [k for k, (low, high) in enumerate(groups) for _ in range(low, high)]
    for j in range(1, ny):
        pltpu.make_async_remote_copy(
            frames.at[0], frames.at[j], send_sem.at[0], frame_sem.at[j], to_y(j), MESH
        ).start()
    for j in range(1, nx):
        pltpu.make_async_remote_copy(
            atoms.at[0], atoms.at[j], send_sem.at[1], atom_sem.at[group_of[j]], to_x(j), MESH
        ).start()

    chunks = KEPT // FB

    def frame_side(s):
        split = jnp.concatenate(pieces(frames[s], 3), axis=0).astype(BF16)
        turned = dot_nt(keep, split).astype(BF16)
        side = dot(turned, fpick).astype(BF16)
        for q in range(chunks):
            for c in range(3):
                lhs[s * chunks + q, c * FB : (c + 1) * FB] = side[
                    q * FB : (q + 1) * FB, c * 128 : c * 128 + DEPTH
                ]

    def atom_side(j):
        split = jnp.concatenate(pieces(atoms[j], 3), axis=0).astype(BF16)
        rhs[j] = dot(apick, split).astype(BF16)

    def pair_block(start, q, segments, sums):
        total = jnp.zeros((FB, 128), F32)
        for k, j in enumerate(segments):
            e = dot(lhs[q], rhs[j])
            e0, e1, e2 = e[:FB], e[FB : 2 * FB], e[2 * FB :]
            y = jnp.minimum((e0 * e0 + e1 * e1) + (e2 * e2 + EPS), 1.0)
            clamped = y * lax.rsqrt(y)
            side = clamped[:, :128] + clamped[:, 128:]
            total = side if k == 0 else total + side
            sums[k] = sums[k] + clamped.reshape(FB // 8, 8, COLS).sum(axis=0)
        acc_f[pl.ds(start, FB)] += total

    def send_sums(segments):
        for j in segments:
            if j:
                pltpu.make_async_remote_copy(
                    asend.at[j], arecv.at[j], send_sem.at[2], sum_sem.at[0], from_x(j), MESH
                ).start()

    nearest = range(first_part)
    frame_side(0)
    atom_side(0)
    all_of(atoms.at[1:first_part], atom_sem.at[0])
    for j in nearest[1:]:
        atom_side(j)
    for j in nearest:
        acc_c[j] = jnp.zeros((8, COLS), F32)

    def one_frame_segment(s, carry):
        @pl.when(s > 0)
        def _():
            all_of(frames.at[s], frame_sem.at[s])
            frame_side(s)

        sums = [acc_c[j] for j in nearest]
        for q in range(chunks):
            start = pl.multiple_of(s * KEPT + q * FB, FB)
            pair_block(start, s * chunks + q, nearest, sums)
        for j in nearest:
            acc_c[j] = sums[j]
        return carry

    lax.fori_loop(0, ny, one_frame_segment, 0)
    running = jnp.zeros((1, COLS), F32)
    for j in nearest:
        asend[j] = acc_c[j].sum(axis=0, keepdims=True)
        running = running + asend[j]
    send_sums(nearest)

    for k, (low, high) in enumerate(groups[1:]):
        segments = range(low, high)
        all_of(atoms.at[low:high], atom_sem.at[k + 1])
        for j in segments:
            atom_side(j)
        sums = [jnp.zeros((8, COLS), F32) for _ in segments]
        for q in range(ny * chunks):
            pair_block(q * FB, q, segments, sums)
        for j, value in zip(segments, sums):
            asend[j] = value.sum(axis=0, keepdims=True)
            running = running + asend[j]
        send_sums(segments)

    frame_flags = frames[0, 12:13]
    for s in range(1, ny):
        frame_flags = frame_flags + frames[s, 12:13]
    tsend[0, 0:1] = running[:, :128] + running[:, 128:]
    tsend[0, 1:2] = frame_flags
    for j in range(1, nx):
        pltpu.make_async_remote_copy(
            tsend.at[0], tsend.at[j], send_sem.at[3], total_sems.at[0], to_x(j), MESH
        ).start()

    ones = jnp.ones((8, 128), BF16)
    weights = jnp.zeros((1, COLS), F32)
    for j in range(nx):
        weights = weights + atoms[j, 6:7]
    psend[...] = jnp.zeros_like(psend)
    for s in range(ny):
        partial = jnp.zeros((8, KEPT), F32)
        for part in pieces(acc_f[s * KEPT : (s + 1) * KEPT], 3):
            partial = partial + dot_nt(ones, part.astype(BF16))
        psend[s, 0:1, 0:KEPT] = partial[0:1]
        psend[s, 1:2] = weights[:, :128] + weights[:, 128:]
        if s:
            pltpu.make_async_remote_copy(
                psend.at[s], precv.at[s], send_sem.at[4], part_sem.at[0], from_y(s), MESH
            ).start()

    all_of(tsend.at[1:nx], total_sems.at[0])
    both = tsend[0]
    for j in range(1, nx):
        both = both + tsend[j]
    usend[0] = both[0:1]
    for j in range(1, ny):
        pltpu.make_async_remote_copy(
            usend.at[0], usend.at[j], send_sem.at[5], total_sems.at[1], to_y(j), MESH
        ).start()
    frame_count = jnp.sum(both[1:2], axis=1, keepdims=True)

    columns = F32(nx * ny * COLS)
    rows = F32(nx * ny * KEPT)
    all_of(precv.at[1:ny], part_sem.at[0])
    mine = psend[0]
    for s in range(1, ny):
        mine = mine + precv[s]
    atom_count = jnp.sum(mine[1:2], axis=1, keepdims=True)
    least_y = jnp.zeros((1, 128), F32) * mine[0:1] + EPS
    least = least_y * lax.rsqrt(least_y)
    own_sum = jnp.zeros((8, FRAMES), F32)
    for part in pieces(jnp.broadcast_to(mine[0:1, :KEPT], (8, KEPT)), 3):
        own_sum = own_sum + dot(part.astype(BF16), keep)
    out_ref[0:1, 0:FRAMES] = (
        frames[0, 12:13] * (own_sum[0:1] - (columns - atom_count) * least) / atom_count
    )
    all_of(arecv.at[1:nx], sum_sem.at[0])
    asum = asend[0]
    for j in range(1, nx):
        asum = asum + arecv[j]
    wide = jnp.concatenate([least, least], axis=1)
    out_ref[1:2, :] = atoms[0, 6:7] * (asum - (rows - frame_count) * wide) / frame_count
    pairs = frame_count * atom_count

    all_of(usend.at[1:ny], total_sems.at[1])
    both = usend[0]
    for j in range(1, ny):
        both = both + usend[j]
    numerator = jnp.sum(both, axis=1, keepdims=True)
    out_ref[2:3, 0:128] = (numerator - least * (rows * columns - pairs)) / pairs

    all_of(frames.at[1:ny], send_sem.at[0])
    all_of(atoms.at[1:nx], send_sem.at[1])
    all_of(arecv.at[1:nx], send_sem.at[2])
    all_of(tsend.at[1:nx], send_sem.at[3])
    all_of(precv.at[1:ny], send_sem.at[4])
    all_of(usend.at[1:ny], send_sem.at[5])


def shards(nx, ny, pred_frames, true_frames, pred_atoms, true_atoms, atom_mask, residue_types, swap_flags):
    dma = pltpu.SemaphoreType.DMA
    blocks = ny * KEPT // FB
    ins = (
        pred_frames, true_frames, pred_atoms, true_atoms, atom_mask.reshape(1, ATOMS),
        residue_types.reshape(1, RESIDUES), swap_flags.reshape(1, RESIDUES), tables(),
    )
    packed = pl.pallas_call(
        functools.partial(kernel, nx, ny),
        out_shape=pltpu.VMEM((8, COLS), F32),
        in_specs=[pl.BlockSpec(memory_space=pl.ANY)] * len(ins),
        out_specs=pl.BlockSpec(memory_space=pltpu.VMEM),
        scratch_shapes=[pltpu.VMEM(a.shape, a.dtype) for a in ins]
        + [
            pltpu.VMEM((8, 128), F32),
            pltpu.VMEM((ny, 16, FRAMES), F32),
            pltpu.VMEM((nx, 8, COLS), F32),
            pltpu.VMEM((blocks, 3 * FB, DEPTH), BF16),
            pltpu.VMEM((nx, DEPTH, COLS), BF16),
            pltpu.VMEM((ny * KEPT, 128), F32),
            pltpu.VMEM((nx, 8, COLS), F32),
            pltpu.VMEM((nx, 1, COLS), F32),
            pltpu.VMEM((nx, 1, COLS), F32),
            pltpu.VMEM((ny, 2, 128), F32),
            pltpu.VMEM((ny, 2, 128), F32),
            pltpu.VMEM((nx, 2, 128), F32),
            pltpu.VMEM((ny, 1, 128), F32),
            dma((len(ins),)), dma((6,)), dma((ny,)), dma((3,)), dma((1,)), dma((1,)), dma((2,)),
        ],
        compiler_params=pltpu.CompilerParams(collective_id=0, has_side_effects=True),
        name="fape",
    )(*ins)
    return packed[0, :FRAMES], packed[1, :ATOMS], packed[2, :1]


def solution(mesh):
    whole = ("sa", "gx", "gy")
    wide, flat = P(None, whole), P(whole)
    return jax.shard_map(
        functools.partial(shards, mesh.shape["gx"], mesh.shape["gy"]),
        mesh=mesh,
        in_specs=(wide, wide, wide, wide, flat, flat, flat),
        out_specs=(flat, flat, P("sa")),
        check_vma=False,
    )
```

```python
import functools

import jax
import jax.numpy as jnp
import numpy as np
from jax import lax
from jax.experimental import pallas as pl
from jax.experimental.pallas import tpu as pltpu
from jax.sharding import PartitionSpec as P

F32 = jnp.float32
BF16 = jnp.bfloat16
MESH = pl.DeviceIdType.MESH

RESIDUES = 16
FRAMES = 8 * RESIDUES
ATOMS = 14 * RESIDUES
KEPT = 6 * RESIDUES
COLS = 256
FB = 32
DEPTH = 32
EPS = 1e-6
ATOM_COUNTS = (5, 11, 8, 8, 6, 9, 9, 4, 10, 8, 8, 9, 8, 11, 7, 6, 7, 14, 12, 7)
CHI_COUNTS = (0, 4, 2, 2, 1, 3, 3, 0, 2, 2, 2, 4, 3, 2, 2, 1, 1, 2, 2, 1)


def tables():
    spread = np.zeros((RESIDUES, 384), np.float32)
    for k in range(ATOMS):
        spread[k // 14, k] = 1.0
    for k in range(FRAMES):
        spread[k // 8, COLS + k] = 1.0
    keep = np.zeros((KEPT, 384), np.float32)
    for k in range(KEPT):
        keep[k, 8 * (k // 6) + (k % 6 + 2 if k % 6 else 0)] = 1.0
    frame_pick = np.zeros((48, 384), np.float32)
    atom_pick = np.zeros((DEPTH, 384), np.float32)
    for c in range(3):
        k = 0
        for i in range(3):
            for cc in range(3):
                if cc == c:
                    frame_pick[12, c * 128 + k] = 1.0
                atom_pick[k, 8 * i + cc] = 1.0
                k += 1
        for j, i in ((0, 0), (0, 1), (0, 2), (1, 0), (1, 1), (2, 0)):
            for b in range(3):
                frame_pick[16 * j + 3 * c + b, c * 128 + k] = 1.0
                atom_pick[k, 8 * i + 3 + b] = 1.0
                k += 1
        for j in range(3):
            frame_pick[16 * j + 9 + c, c * 128 + k] = 1.0
            atom_pick[k, 6] = 1.0
            k += 1
    return jnp.asarray(np.concatenate([spread, keep, frame_pick, atom_pick]), BF16)


def dot(a, b):
    return jnp.dot(a, b, preferred_element_type=F32)


def dot_nt(a, b):
    return lax.dot_general(a, b, (((1,), (1,)), ((), ())), preferred_element_type=F32)


def pieces(x, count):
    parts = []
    for _ in range(count):
        part = x.astype(BF16).astype(F32)
        parts.append(part)
        x = x - part
    return parts


def by_type(types, values):
    total = jnp.zeros(types.shape, F32)
    for k, value in enumerate(values):
        total = jnp.where(types == k, F32(value), total)
    return total


def all_of(ref, sem):
    pltpu.make_async_copy(ref, ref, sem).wait()


def kernel(
    nx, ny, tiles,
    pf_hbm, tf_hbm, pa_hbm, ta_hbm, mask_hbm, type_hbm, swap_hbm, consts_hbm,
    out_ref,
    pf, tf, pa, ta, mask, types, swaps, consts,
    res, frames, atoms, lhs, rhs, acc_f, packed, unpacked,
    asend, arecv, psend, precv, tsend, usend,
    in_sem, send_sem, frame_sem, atom_sem, sum_sem, part_sem, total_sems,
):
    gx, gy = lax.axis_index("gx"), lax.axis_index("gy")
    nz, nw, part = nx // 2, ny // 2, nx // 2
    z, core, w, half = lax.div(gx, 2), lax.rem(gx, 2), lax.div(gy, 2), lax.rem(gy, 2)
    near_z = [0] + [d for k in range(1, nz // 2 + 1) for d in sorted({k, nz - k})]
    near_w = [0] + [d for k in range(1, nw // 2 + 1) for d in sorted({k, nw - k})]

    def to_x(j):
        return {"gx": 2 * lax.rem(z + near_z[j // 2], nz) + lax.rem(core + j % 2, 2)}

    def from_x(j):
        return {"gx": 2 * lax.rem(z + nz - near_z[j // 2], nz) + lax.rem(core + j % 2, 2)}

    def to_y(j):
        return {"gy": 2 * lax.rem(w + near_w[j % nw], nw) + lax.rem(half + j // nw, 2)}

    def from_y(j):
        return {"gy": 2 * lax.rem(w + nw - near_w[j % nw], nw) + lax.rem(half + j // nw, 2)}

    for j in range(nx):
        atoms[j, 7:8] = jnp.zeros((1, COLS), F32)
    for j in range(ny):
        frames[j, 13:16] = jnp.zeros((3, FRAMES), F32)
    barrier = pltpu.get_barrier_semaphore()
    for j in range(1, nx):
        pl.semaphore_signal(barrier, inc=1, device_id=to_x(j), device_id_type=MESH)
    for j in range(1, ny):
        pl.semaphore_signal(barrier, inc=1, device_id=to_y(j), device_id_type=MESH)

    loads = [
        pltpu.make_async_copy(src, dst, in_sem.at[k])
        for k, (src, dst) in enumerate(
            (
                (type_hbm, types), (swap_hbm, swaps), (consts_hbm, consts), (pf_hbm, pf),
                (tf_hbm, tf), (pa_hbm, pa), (ta_hbm, ta), (mask_hbm, mask),
            )
        )
    ]
    for load in loads:
        load.start()
    res[...] = jnp.zeros_like(res)
    atoms[0] = jnp.zeros((8, COLS), F32)
    acc_f[...] = jnp.zeros_like(acc_f)
    asend[...] = jnp.zeros_like(asend)
    if part * ATOMS != tiles * COLS:
        packed[...] = jnp.zeros_like(packed)
    for load in loads:
        load.wait()
    spread = consts[0:RESIDUES]
    keep = consts[RESIDUES : RESIDUES + KEPT, 0:128]
    fpick = consts[RESIDUES + KEPT : RESIDUES + KEPT + 48]
    apick = consts[RESIDUES + KEPT + 48 : RESIDUES + KEPT + 48 + DEPTH, 0:24]

    kind, swap = types[...], swaps[...] == 1
    first = (kind == 3) | (kind == 13) | (kind == 18)
    third = (kind == 13) | (kind == 18)
    res[0:1, 0:RESIDUES] = by_type(kind, ATOM_COUNTS)
    res[1:2, 0:RESIDUES] = by_type(kind, CHI_COUNTS)
    res[2:3, 0:RESIDUES] = jnp.where(first & swap, F32(1), F32(0))
    res[3:4, 0:RESIDUES] = jnp.where((kind == 6) & swap, F32(1), F32(0))
    res[4:5, 0:RESIDUES] = jnp.where(third & swap, F32(1), F32(0))
    of_both = dot(res[:, 0:RESIDUES].astype(BF16), spread)
    of_atom, of_frame = of_both[:, :COLS], of_both[:, COLS:]

    lane = lax.broadcasted_iota(jnp.int32, (1, COLS), 1)
    slot = lane - 14 * ((lane * 4682) >> 16)
    swap_a, swap_b, swap_c = (of_atom[k : k + 1] > 0.5 for k in (2, 3, 4))
    upper = ((slot == 6) & swap_a) | ((slot == 7) & swap_b) | ((slot == 8) & swap_c)
    lower = ((slot == 7) & swap_a) | ((slot == 8) & swap_b) | ((slot == 9) & swap_c)
    atoms[0, 0:3, 0:ATOMS] = pa[...]
    atoms[0, 3:6, 0:ATOMS] = ta[...]
    atoms[0, 6:7, 0:ATOMS] = mask[...].astype(F32)
    raw = atoms[0]
    row = lax.broadcasted_iota(jnp.int32, (8, COLS), 0)
    renamed = jnp.where(
        upper & (row >= 3), pltpu.roll(raw, COLS - 1, 1),
        jnp.where(lower & (row >= 3), pltpu.roll(raw, 1, 1), raw),
    )
    weight = jnp.where(slot.astype(F32) < of_atom[0:1], renamed[6:7], F32(0))
    atoms[0] = renamed * jnp.where(row < 3, F32(0.1), F32(1.0)) * weight

    group = lax.broadcasted_iota(jnp.int32, (1, FRAMES), 1) & 7
    exists = jnp.where(
        (group == 0) | (group == 3) | ((group >= 4) & ((group - 3).astype(F32) <= of_frame[1:2])),
        F32(1), F32(0),
    )
    flips = ((group == 5) & (of_frame[2:3] > 0.5)) | ((group == 6) & (of_frame[3:4] > 0.5))
    sign = jnp.where(flips, F32(-1), F32(1))
    rot_p = [pf[k : k + 1] for k in range(12)]
    rot_t = [tf[k : k + 1] * sign if k % 3 and k < 9 else tf[k : k + 1] for k in range(12)]
    scale = -0.1 * exists
    for a in range(3):
        moved = rot_p[9 + a] * scale
        for b in range(3):
            turn = scale * (
                rot_p[3 * a] * rot_t[3 * b]
                + rot_p[3 * a + 1] * rot_t[3 * b + 1]
                + rot_p[3 * a + 2] * rot_t[3 * b + 2]
            )
            frames[0, 3 * a + b : 3 * a + b + 1] = turn
            moved = moved - turn * rot_t[9 + b]
        frames[0, 9 + a : 10 + a] = moved
    frames[0, 12:13] = exists

    pl.semaphore_wait(barrier, nx - 1 + ny - 1)

    def send_atoms(j):
        pltpu.make_async_remote_copy(
            atoms.at[0, 0:7], atoms.at[j, 0:7], send_sem.at[1], atom_sem.at[j // part],
            to_x(j), MESH,
        ).start()

    for j in range(1, part):
        send_atoms(j)
    for j in range(1, ny):
        pltpu.make_async_remote_copy(
            frames.at[0, 0:13], frames.at[j, 0:13], send_sem.at[0], frame_sem.at[j],
            to_y(j), MESH,
        ).start()
    for j in range(part, nx):
        send_atoms(j)

    chunks = KEPT // FB

    def frame_side(s):
        split = jnp.concatenate(pieces(frames[s], 3), axis=0).astype(BF16)
        turned = dot_nt(keep, split).astype(BF16)
        side = dot(turned, fpick).astype(BF16)
        for q in range(chunks):
            for c in range(3):
                lhs[s * chunks + q, c * FB : (c + 1) * FB] = side[
                    q * FB : (q + 1) * FB, c * 128 : c * 128 + DEPTH
                ]

    def atom_side(group):
        for k in range(part):
            packed[:, k * ATOMS : (k + 1) * ATOMS] = atoms[group * part + k, :, 0:ATOMS]
        split = jnp.concatenate(pieces(packed[...], 3), axis=0).astype(BF16)
        side = dot(apick, split).astype(BF16)
        for t in range(tiles):
            rhs[group * tiles + t] = side[:, t * COLS : (t + 1) * COLS]

    def pair_block(start, q, segments, sums):
        total = jnp.zeros((FB, 128), F32)
        for k, j in enumerate(segments):
            e = dot(lhs[q], rhs[j])
            e0, e1, e2 = e[:FB], e[FB : 2 * FB], e[2 * FB :]
            y = jnp.minimum((e0 * e0 + e1 * e1) + (e2 * e2 + EPS), 1.0)
            clamped = y * lax.rsqrt(y)
            side = clamped[:, :128] + clamped[:, 128:]
            total = side if k == 0 else total + side
            sums[k] = sums[k] + clamped.reshape(FB // 8, 8, COLS).sum(axis=0)
        acc_f[pl.ds(start, FB)] += total

    def send_sums(group, sums):
        total = jnp.zeros((1, COLS), F32)
        for t, value in enumerate(sums):
            row = value.sum(axis=0, keepdims=True)
            unpacked[0:1, t * COLS : (t + 1) * COLS] = row
            total = total + row
        for k in range(part):
            j = group * part + k
            asend[j, :, 0:ATOMS] = unpacked[0:1, k * ATOMS : (k + 1) * ATOMS]
            if j:
                pltpu.make_async_remote_copy(
                    asend.at[j], arecv.at[j], send_sem.at[2], sum_sem.at[0], from_x(j), MESH
                ).start()
        return total

    def wait_frames(s):
        all_of(frames.at[s, 0:13], frame_sem.at[s])
        frame_side(s)

    near = ny // 2 + 1
    frame_side(0)
    all_of(atoms.at[1:part, 0:7], atom_sem.at[0])
    atom_side(0)
    for s in range(1, near):
        wait_frames(s)
    sums = [jnp.zeros((8, COLS), F32) for _ in range(tiles)]
    for q in range(near * chunks):
        pair_block(q * FB, q, range(tiles), sums)
    for s in range(near, ny):
        wait_frames(s)
    for q in range(near * chunks, ny * chunks):
        pair_block(q * FB, q, range(tiles), sums)
    running = send_sums(0, sums)
    all_of(atoms.at[part:nx, 0:7], atom_sem.at[1])
    atom_side(1)
    sums = [jnp.zeros((8, COLS), F32) for _ in range(tiles)]
    for q in range(ny * chunks):
        pair_block(q * FB, q, range(tiles, 2 * tiles), sums)
    running = running + send_sums(1, sums)

    frame_flags = frames[0, 12:13]
    for s in range(1, ny):
        frame_flags = frame_flags + frames[s, 12:13]
    tsend[0, 0:1] = running[:, :128] + running[:, 128:]
    tsend[0, 1:2] = frame_flags
    for j in range(1, nx):
        pltpu.make_async_remote_copy(
            tsend.at[0], tsend.at[j], send_sem.at[3], total_sems.at[0], to_x(j), MESH
        ).start()

    ones = jnp.ones((8, 128), BF16)
    weights = jnp.zeros((1, COLS), F32)
    for j in range(nx):
        weights = weights + atoms[j, 6:7]
    psend[...] = jnp.zeros_like(psend)
    for s in range(ny):
        partial = jnp.zeros((8, KEPT), F32)
        for part in pieces(acc_f[s * KEPT : (s + 1) * KEPT], 3):
            partial = partial + dot_nt(ones, part.astype(BF16))
        psend[s, 0:1, 0:KEPT] = partial[0:1]
        psend[s, 1:2] = weights[:, :128] + weights[:, 128:]
        if s:
            pltpu.make_async_remote_copy(
                psend.at[s], precv.at[s], send_sem.at[4], part_sem.at[0], from_y(s), MESH
            ).start()

    all_of(tsend.at[1:nx], total_sems.at[0])
    both = tsend[0]
    for j in range(1, nx):
        both = both + tsend[j]
    usend[0] = both[0:1]
    for j in range(1, ny):
        pltpu.make_async_remote_copy(
            usend.at[0], usend.at[j], send_sem.at[5], total_sems.at[1], to_y(j), MESH
        ).start()
    frame_count = jnp.sum(both[1:2], axis=1, keepdims=True)

    columns = F32(2 * tiles * ny * COLS)
    rows = F32(nx * ny * KEPT)
    all_of(precv.at[1:ny], part_sem.at[0])
    mine = psend[0]
    for s in range(1, ny):
        mine = mine + precv[s]
    atom_count = jnp.sum(mine[1:2], axis=1, keepdims=True)
    least_y = jnp.zeros((1, 128), F32) * mine[0:1] + EPS
    least = least_y * lax.rsqrt(least_y)
    own_sum = jnp.zeros((8, FRAMES), F32)
    for part in pieces(jnp.broadcast_to(mine[0:1, :KEPT], (8, KEPT)), 3):
        own_sum = own_sum + dot(part.astype(BF16), keep)
    out_ref[0:1, 0:FRAMES] = (
        frames[0, 12:13] * (own_sum[0:1] - (columns - atom_count) * least) / atom_count
    )
    all_of(arecv.at[1:nx], sum_sem.at[0])
    asum = asend[0]
    for j in range(1, nx):
        asum = asum + arecv[j]
    wide = jnp.concatenate([least, least], axis=1)
    out_ref[1:2, :] = atoms[0, 6:7] * (asum - (rows - frame_count) * wide) / frame_count
    pairs = frame_count * atom_count

    all_of(usend.at[1:ny], total_sems.at[1])
    both = usend[0]
    for j in range(1, ny):
        both = both + usend[j]
    numerator = jnp.sum(both, axis=1, keepdims=True)
    out_ref[2:3, 0:128] = (numerator - least * (rows * columns - pairs)) / pairs

    all_of(frames.at[1:ny, 0:13], send_sem.at[0])
    all_of(atoms.at[1:nx, 0:7], send_sem.at[1])
    all_of(arecv.at[1:nx], send_sem.at[2])
    all_of(tsend.at[1:nx], send_sem.at[3])
    all_of(precv.at[1:ny], send_sem.at[4])
    all_of(usend.at[1:ny], send_sem.at[5])


def shards(nx, ny, pred_frames, true_frames, pred_atoms, true_atoms, atom_mask, residue_types, swap_flags):
    dma = pltpu.SemaphoreType.DMA
    blocks = ny * KEPT // FB
    tiles = -(-nx // 2 * ATOMS // COLS)
    ins = (
        pred_frames, true_frames, pred_atoms, true_atoms, atom_mask.reshape(1, ATOMS),
        residue_types.reshape(1, RESIDUES), swap_flags.reshape(1, RESIDUES), tables(),
    )
    packed = pl.pallas_call(
        functools.partial(kernel, nx, ny, tiles),
        out_shape=pltpu.VMEM((8, COLS), F32),
        in_specs=[pl.BlockSpec(memory_space=pl.ANY)] * len(ins),
        out_specs=pl.BlockSpec(memory_space=pltpu.VMEM),
        scratch_shapes=[pltpu.VMEM(a.shape, a.dtype) for a in ins]
        + [
            pltpu.VMEM((8, 128), F32),
            pltpu.VMEM((ny, 16, FRAMES), F32),
            pltpu.VMEM((nx, 8, COLS), F32),
            pltpu.VMEM((blocks, 3 * FB, DEPTH), BF16),
            pltpu.VMEM((2 * tiles, DEPTH, COLS), BF16),
            pltpu.VMEM((ny * KEPT, 128), F32),
            pltpu.VMEM((8, tiles * COLS), F32),
            pltpu.VMEM((8, tiles * COLS), F32),
            pltpu.VMEM((nx, 1, COLS), F32),
            pltpu.VMEM((nx, 1, COLS), F32),
            pltpu.VMEM((ny, 2, 128), F32),
            pltpu.VMEM((ny, 2, 128), F32),
            pltpu.VMEM((nx, 2, 128), F32),
            pltpu.VMEM((ny, 1, 128), F32),
            dma((len(ins),)), dma((6,)), dma((ny,)), dma((2,)), dma((1,)), dma((1,)), dma((2,)),
        ],
        compiler_params=pltpu.CompilerParams(collective_id=0, has_side_effects=True),
        name="fape",
    )(*ins)
    return packed[0, :FRAMES], packed[1, :ATOMS], packed[2, :1]


def solution(mesh):
    whole = ("sa", "gx", "gy")
    wide, flat = P(None, whole), P(whole)
    return jax.shard_map(
        functools.partial(shards, mesh.shape["gx"], mesh.shape["gy"]),
        mesh=mesh,
        in_specs=(wide, wide, wide, wide, flat, flat, flat),
        out_specs=(flat, flat, P("sa")),
        check_vma=False,
    )
```

```python
import functools

import jax
import jax.numpy as jnp
import numpy as np
from jax import lax
from jax.experimental import pallas as pl
from jax.experimental.pallas import tpu as pltpu
from jax.sharding import PartitionSpec as P

F32 = jnp.float32
BF16 = jnp.bfloat16
MESH = pl.DeviceIdType.MESH

RESIDUES = 16
FRAMES = 8 * RESIDUES
ATOMS = 14 * RESIDUES
KEPT = 6 * RESIDUES
COLS = 256
FB = 32
DEPTH = 32
EPS = 1e-6
ATOM_COUNTS = (5, 11, 8, 8, 6, 9, 9, 4, 10, 8, 8, 9, 8, 11, 7, 6, 7, 14, 12, 7)
CHI_COUNTS = (0, 4, 2, 2, 1, 3, 3, 0, 2, 2, 2, 4, 3, 2, 2, 1, 1, 2, 2, 1)


def tables():
    spread = np.zeros((RESIDUES, 384), np.float32)
    for k in range(ATOMS):
        spread[k // 14, k] = 1.0
    for k in range(FRAMES):
        spread[k // 8, COLS + k] = 1.0
    keep = np.zeros((KEPT, 384), np.float32)
    for k in range(KEPT):
        keep[k, 8 * (k // 6) + (k % 6 + 2 if k % 6 else 0)] = 1.0
    frame_pick = np.zeros((48, 384), np.float32)
    atom_pick = np.zeros((DEPTH, 384), np.float32)
    for c in range(3):
        k = 0
        for i in range(3):
            for cc in range(3):
                if cc == c:
                    frame_pick[12, c * 128 + k] = 1.0
                atom_pick[k, 8 * i + cc] = 1.0
                k += 1
        for j, i in ((0, 0), (0, 1), (0, 2), (1, 0), (1, 1), (2, 0)):
            for b in range(3):
                frame_pick[16 * j + 3 * c + b, c * 128 + k] = 1.0
                atom_pick[k, 8 * i + 3 + b] = 1.0
                k += 1
        for j in range(3):
            frame_pick[16 * j + 9 + c, c * 128 + k] = 1.0
            atom_pick[k, 6] = 1.0
            k += 1
    return jnp.asarray(np.concatenate([spread, keep, frame_pick, atom_pick]), BF16)


def dot(a, b):
    return jnp.dot(a, b, preferred_element_type=F32)


def dot_nt(a, b):
    return lax.dot_general(a, b, (((1,), (1,)), ((), ())), preferred_element_type=F32)


def pieces(x, count):
    parts = []
    for _ in range(count):
        part = x.astype(BF16).astype(F32)
        parts.append(part)
        x = x - part
    return parts


def by_type(types, values):
    total = jnp.zeros(types.shape, F32)
    for k, value in enumerate(values):
        total = jnp.where(types == k, F32(value), total)
    return total


def all_of(ref, sem):
    pltpu.make_async_copy(ref, ref, sem).wait()


def kernel(
    nx, ny, tiles,
    pf_hbm, tf_hbm, pa_hbm, ta_hbm, mask_hbm, type_hbm, swap_hbm, consts_hbm,
    out_ref,
    pf, tf, pa, ta, mask, types, swaps, consts,
    res, frames, atoms, lhs, rhs, acc_f, packed, unpacked,
    asend, arecv, psend, precv, totals,
    in_sem, send_sem, frame_sem, atom_sem, sum_sem, part_sem, total_sem,
):
    gx, gy = lax.axis_index("gx"), lax.axis_index("gy")
    nz, nw, part = nx // 2, ny // 2, nx // 2
    z, core, w, half = lax.div(gx, 2), lax.rem(gx, 2), lax.div(gy, 2), lax.rem(gy, 2)
    near_z = [0] + [d for k in range(1, nz // 2 + 1) for d in sorted({k, nz - k})]
    near_w = [0] + [d for k in range(1, nw // 2 + 1) for d in sorted({k, nw - k})]

    def to_x(j):
        return {"gx": 2 * lax.rem(z + near_z[j // 2], nz) + lax.rem(core + j % 2, 2)}

    def from_x(j):
        return {"gx": 2 * lax.rem(z + nz - near_z[j // 2], nz) + lax.rem(core + j % 2, 2)}

    def to_y(j):
        return {"gy": 2 * lax.rem(w + near_w[j % nw], nw) + lax.rem(half + j // nw, 2)}

    def from_y(j):
        return {"gy": 2 * lax.rem(w + nw - near_w[j % nw], nw) + lax.rem(half + j // nw, 2)}

    for j in range(nx):
        atoms[j, 7:8] = jnp.zeros((1, COLS), F32)
    for j in range(ny):
        frames[j, 13:16] = jnp.zeros((3, FRAMES), F32)
    barrier = pltpu.get_barrier_semaphore()
    for j in range(1, nx):
        pl.semaphore_signal(barrier, inc=1, device_id=to_x(j), device_id_type=MESH)
    for j in range(1, ny):
        pl.semaphore_signal(barrier, inc=1, device_id=to_y(j), device_id_type=MESH)

    loads = [
        pltpu.make_async_copy(src, dst, in_sem.at[k])
        for k, (src, dst) in enumerate(
            (
                (type_hbm, types), (swap_hbm, swaps), (consts_hbm, consts), (pf_hbm, pf),
                (tf_hbm, tf), (pa_hbm, pa), (ta_hbm, ta), (mask_hbm, mask),
            )
        )
    ]
    for load in loads:
        load.start()
    res[...] = jnp.zeros_like(res)
    atoms[0] = jnp.zeros((8, COLS), F32)
    acc_f[...] = jnp.zeros_like(acc_f)
    asend[...] = jnp.zeros_like(asend)
    psend[...] = jnp.zeros_like(psend)
    if part * ATOMS != tiles * COLS:
        packed[...] = jnp.zeros_like(packed)
    for load in loads:
        load.wait()
    spread = consts[0:RESIDUES]
    keep = consts[RESIDUES : RESIDUES + KEPT, 0:128]
    fpick = consts[RESIDUES + KEPT : RESIDUES + KEPT + 48]
    apick = consts[RESIDUES + KEPT + 48 : RESIDUES + KEPT + 48 + DEPTH, 0:24]

    kind, swap = types[...], swaps[...] == 1
    first = (kind == 3) | (kind == 13) | (kind == 18)
    third = (kind == 13) | (kind == 18)
    res[0:1, 0:RESIDUES] = by_type(kind, ATOM_COUNTS)
    res[1:2, 0:RESIDUES] = by_type(kind, CHI_COUNTS)
    res[2:3, 0:RESIDUES] = jnp.where(first & swap, F32(1), F32(0))
    res[3:4, 0:RESIDUES] = jnp.where((kind == 6) & swap, F32(1), F32(0))
    res[4:5, 0:RESIDUES] = jnp.where(third & swap, F32(1), F32(0))
    of_both = dot(res[:, 0:RESIDUES].astype(BF16), spread)
    of_atom, of_frame = of_both[:, :COLS], of_both[:, COLS:]

    lane = lax.broadcasted_iota(jnp.int32, (1, COLS), 1)
    slot = lane - 14 * ((lane * 4682) >> 16)
    swap_a, swap_b, swap_c = (of_atom[k : k + 1] > 0.5 for k in (2, 3, 4))
    upper = ((slot == 6) & swap_a) | ((slot == 7) & swap_b) | ((slot == 8) & swap_c)
    lower = ((slot == 7) & swap_a) | ((slot == 8) & swap_b) | ((slot == 9) & swap_c)
    atoms[0, 0:3, 0:ATOMS] = pa[...]
    atoms[0, 3:6, 0:ATOMS] = ta[...]
    atoms[0, 6:7, 0:ATOMS] = mask[...].astype(F32)
    raw = atoms[0]
    row = lax.broadcasted_iota(jnp.int32, (8, COLS), 0)
    renamed = jnp.where(
        upper & (row >= 3), pltpu.roll(raw, COLS - 1, 1),
        jnp.where(lower & (row >= 3), pltpu.roll(raw, 1, 1), raw),
    )
    weight = jnp.where(slot.astype(F32) < of_atom[0:1], renamed[6:7], F32(0))
    atoms[0] = renamed * jnp.where(row < 3, F32(0.1), F32(1.0)) * weight

    group = lax.broadcasted_iota(jnp.int32, (1, FRAMES), 1) & 7
    exists = jnp.where(
        (group == 0) | (group == 3) | ((group >= 4) & ((group - 3).astype(F32) <= of_frame[1:2])),
        F32(1), F32(0),
    )
    flips = ((group == 5) & (of_frame[2:3] > 0.5)) | ((group == 6) & (of_frame[3:4] > 0.5))
    sign = jnp.where(flips, F32(-1), F32(1))
    rot_p = [pf[k : k + 1] for k in range(12)]
    rot_t = [tf[k : k + 1] * sign if k % 3 and k < 9 else tf[k : k + 1] for k in range(12)]
    scale = -0.1 * exists
    for a in range(3):
        moved = rot_p[9 + a] * scale
        for b in range(3):
            turn = scale * (
                rot_p[3 * a] * rot_t[3 * b]
                + rot_p[3 * a + 1] * rot_t[3 * b + 1]
                + rot_p[3 * a + 2] * rot_t[3 * b + 2]
            )
            frames[0, 3 * a + b : 3 * a + b + 1] = turn
            moved = moved - turn * rot_t[9 + b]
        frames[0, 9 + a : 10 + a] = moved
    frames[0, 12:13] = exists

    pl.semaphore_wait(barrier, nx - 1 + ny - 1)

    def send_atoms(j):
        pltpu.make_async_remote_copy(
            atoms.at[0, 0:7], atoms.at[j, 0:7], send_sem.at[1], atom_sem.at[j // part],
            to_x(j), MESH,
        ).start()

    for j in range(1, part):
        send_atoms(j)
    for j in range(1, ny):
        pltpu.make_async_remote_copy(
            frames.at[0, 0:13], frames.at[j, 0:13], send_sem.at[0], frame_sem.at[j],
            to_y(j), MESH,
        ).start()
    for j in range(part, nx):
        send_atoms(j)

    chunks = KEPT // FB

    def frame_side(s):
        split = jnp.concatenate(pieces(frames[s], 3), axis=0).astype(BF16)
        turned = dot_nt(keep, split).astype(BF16)
        side = dot(turned, fpick).astype(BF16)
        for q in range(chunks):
            for c in range(3):
                lhs[s * chunks + q, c * FB : (c + 1) * FB] = side[
                    q * FB : (q + 1) * FB, c * 128 : c * 128 + DEPTH
                ]

    def atom_side(group):
        for k in range(part):
            packed[:, k * ATOMS : (k + 1) * ATOMS] = atoms[group * part + k, :, 0:ATOMS]
        split = jnp.concatenate(pieces(packed[...], 3), axis=0).astype(BF16)
        side = dot(apick, split).astype(BF16)
        for t in range(tiles):
            rhs[group * tiles + t] = side[:, t * COLS : (t + 1) * COLS]

    def pair_block(start, q, segments, sums):
        total = jnp.zeros((FB, 128), F32)
        for k, j in enumerate(segments):
            e = dot(lhs[q], rhs[j])
            e0, e1, e2 = e[:FB], e[FB : 2 * FB], e[2 * FB :]
            y = jnp.minimum((e0 * e0 + e1 * e1) + (e2 * e2 + EPS), 1.0)
            clamped = y * lax.rsqrt(y)
            side = clamped[:, :128] + clamped[:, 128:]
            total = side if k == 0 else total + side
            sums[k] = sums[k] + clamped.reshape(FB // 8, 8, COLS).sum(axis=0)
        acc_f[pl.ds(start, FB)] += total

    def column_rows(sums):
        total = jnp.zeros((1, COLS), F32)
        for t, value in enumerate(sums):
            row = value.sum(axis=0, keepdims=True)
            unpacked[0:1, t * COLS : (t + 1) * COLS] = row
            total = total + row
        return total

    def send_sums(group, frame_flags):
        for k in range(part):
            j = group * part + k
            asend[j, :, 0:ATOMS] = unpacked[0:1, k * ATOMS : (k + 1) * ATOMS]
            asend[j, :, ATOMS : ATOMS + 1] = frame_flags
        for j in range(max(1, group * part), (group + 1) * part):
            pltpu.make_async_remote_copy(
                asend.at[j], arecv.at[j], send_sem.at[2], sum_sem.at[0], from_x(j), MESH
            ).start()

    def wait_frames(low, high):
        for s in range(low, high):
            all_of(frames.at[s, 0:13], frame_sem.at[s])
        for s in range(low, high):
            frame_side(s)

    near = ny // 2 + 1
    frame_side(0)
    all_of(atoms.at[1:part, 0:7], atom_sem.at[0])
    wait_frames(1, near)
    atom_side(0)
    sums = [jnp.zeros((8, COLS), F32) for _ in range(tiles)]
    for q in range(near * chunks):
        pair_block(q * FB, q, range(tiles), sums)
    wait_frames(near, ny)
    for q in range(near * chunks, ny * chunks):
        pair_block(q * FB, q, range(tiles), sums)
    all_of(atoms.at[part:nx, 0:7], atom_sem.at[1])
    atom_side(1)
    flags = frames[0, 12:13]
    for s in range(1, ny):
        flags = flags + frames[s, 12:13]
    flags = jnp.sum(flags, axis=1, keepdims=True)
    running = column_rows(sums)
    send_sums(0, flags)
    sums = [jnp.zeros((8, COLS), F32) for _ in range(tiles)]
    for q in range(ny * chunks):
        pair_block(q * FB, q, range(tiles, 2 * tiles), sums)
    running = running + column_rows(sums)

    def hops(jx, jy):
        dz, dw = near_z[jx // 2], near_w[jy % nw]
        return min(dz, nz - dz) + min(dw, nw - dw) + 2 * (jy // nw)

    others = sorted(
        ((jx, jy) for jx in range(nx) for jy in range(ny) if jx or jy), key=lambda j: -hops(*j)
    )

    def send_total(jx, jy):
        k = jx * ny + jy
        pltpu.make_async_remote_copy(
            totals.at[0:1], totals.at[k : k + 1], send_sem.at[3], total_sem.at[0],
            {**to_x(jx), **to_y(jy)}, MESH,
        ).start()

    totals[0:1] = running[:, :128] + running[:, 128:]
    first_sent = len(others) // 2
    for j in others[:first_sent]:
        send_total(*j)
    send_sums(1, flags)

    ones = jnp.ones((8, 128), BF16)
    weights = jnp.zeros((1, COLS), F32)
    for j in range(nx):
        weights = weights + atoms[j, 6:7]
    weights = jnp.sum(weights, axis=1, keepdims=True)
    for s in range(ny):
        partial = jnp.zeros((8, KEPT), F32)
        for piece in pieces(acc_f[s * KEPT : (s + 1) * KEPT], 3):
            partial = partial + dot_nt(ones, piece.astype(BF16))
        psend[s, :, 0:KEPT] = partial[0:1]
        psend[s, :, KEPT : KEPT + 1] = weights
    for s in range(1, ny):
        pltpu.make_async_remote_copy(
            psend.at[s], precv.at[s], send_sem.at[4], part_sem.at[0], from_y(s), MESH
        ).start()
    for j in others[first_sent:]:
        send_total(*j)

    columns = F32(2 * tiles * ny * COLS)
    rows = F32(nx * ny * KEPT)
    all_of(precv.at[1:ny], part_sem.at[0])
    mine = psend[0]
    for s in range(1, ny):
        mine = mine + precv[s]
    atom_count = mine[:, KEPT : KEPT + 1]
    least_y = jnp.zeros((1, 128), F32) * mine + EPS
    least = least_y * lax.rsqrt(least_y)
    own_sum = jnp.zeros((8, FRAMES), F32)
    for piece in pieces(jnp.broadcast_to(mine[:, :KEPT], (8, KEPT)), 3):
        own_sum = own_sum + dot(piece.astype(BF16), keep)
    out_ref[0:1, 0:FRAMES] = (
        frames[0, 12:13] * (own_sum[0:1] - (columns - atom_count) * least) / atom_count
    )
    all_of(arecv.at[1:nx], sum_sem.at[0])
    asum = asend[0]
    for j in range(1, nx):
        asum = asum + arecv[j]
    frame_count = asum[:, ATOMS : ATOMS + 1]
    wide = jnp.concatenate([least, least], axis=1)
    out_ref[1:2, :] = atoms[0, 6:7] * (asum - (rows - frame_count) * wide) / frame_count
    pairs = frame_count * atom_count

    all_of(totals.at[1 : nx * ny], total_sem.at[0])
    numerator = jnp.sum(
        jnp.sum(totals[...], axis=0, keepdims=True), axis=1, keepdims=True
    )
    out_ref[2:3, 0:128] = (numerator - least * (rows * columns - pairs)) / pairs

    all_of(frames.at[1:ny, 0:13], send_sem.at[0])
    all_of(atoms.at[1:nx, 0:7], send_sem.at[1])
    all_of(arecv.at[1:nx], send_sem.at[2])
    all_of(totals.at[1 : nx * ny], send_sem.at[3])
    all_of(precv.at[1:ny], send_sem.at[4])


def shards(nx, ny, pred_frames, true_frames, pred_atoms, true_atoms, atom_mask, residue_types, swap_flags):
    dma = pltpu.SemaphoreType.DMA
    blocks = ny * KEPT // FB
    tiles = -(-nx // 2 * ATOMS // COLS)
    ins = (
        pred_frames, true_frames, pred_atoms, true_atoms, atom_mask.reshape(1, ATOMS),
        residue_types.reshape(1, RESIDUES), swap_flags.reshape(1, RESIDUES), tables(),
    )
    packed = pl.pallas_call(
        functools.partial(kernel, nx, ny, tiles),
        out_shape=pltpu.VMEM((8, COLS), F32),
        in_specs=[pl.BlockSpec(memory_space=pl.ANY)] * len(ins),
        out_specs=pl.BlockSpec(memory_space=pltpu.VMEM),
        scratch_shapes=[pltpu.VMEM(a.shape, a.dtype) for a in ins]
        + [
            pltpu.VMEM((8, 128), F32),
            pltpu.VMEM((ny, 16, FRAMES), F32),
            pltpu.VMEM((nx, 8, COLS), F32),
            pltpu.VMEM((blocks, 3 * FB, DEPTH), BF16),
            pltpu.VMEM((2 * tiles, DEPTH, COLS), BF16),
            pltpu.VMEM((ny * KEPT, 128), F32),
            pltpu.VMEM((8, tiles * COLS), F32),
            pltpu.VMEM((8, tiles * COLS), F32),
            pltpu.VMEM((nx, 1, COLS), F32),
            pltpu.VMEM((nx, 1, COLS), F32),
            pltpu.VMEM((ny, 1, 128), F32),
            pltpu.VMEM((ny, 1, 128), F32),
            pltpu.VMEM((nx * ny, 128), F32),
            dma((len(ins),)), dma((5,)), dma((ny,)), dma((2,)), dma((1,)), dma((1,)), dma((1,)),
        ],
        compiler_params=pltpu.CompilerParams(collective_id=0, has_side_effects=True),
        name="fape",
    )(*ins)
    return packed[0, :FRAMES], packed[1, :ATOMS], packed[2, :1]


def solution(mesh):
    whole = ("sa", "gx", "gy")
    wide, flat = P(None, whole), P(whole)
    return jax.shard_map(
        functools.partial(shards, mesh.shape["gx"], mesh.shape["gy"]),
        mesh=mesh,
        in_specs=(wide, wide, wide, wide, flat, flat, flat),
        out_specs=(flat, flat, P("sa")),
        check_vma=False,
    )
```

```python
import functools

import jax
import jax.numpy as jnp
import numpy as np
from jax import lax
from jax.experimental import pallas as pl
from jax.experimental.pallas import tpu as pltpu
from jax.sharding import PartitionSpec as P

F32 = jnp.float32
BF16 = jnp.bfloat16
MESH = pl.DeviceIdType.MESH

RESIDUES = 16
FRAMES = 8 * RESIDUES
ATOMS = 14 * RESIDUES
KEPT = 6 * RESIDUES
COLS = 256
FB = 32
DEPTH = 32
EPS = 1e-6
ATOM_COUNTS = (5, 11, 8, 8, 6, 9, 9, 4, 10, 8, 8, 9, 8, 11, 7, 6, 7, 14, 12, 7)
CHI_COUNTS = (0, 4, 2, 2, 1, 3, 3, 0, 2, 2, 2, 4, 3, 2, 2, 1, 1, 2, 2, 1)


def tables():
    spread = np.zeros((RESIDUES, 384), np.float32)
    for k in range(ATOMS):
        spread[k // 14, k] = 1.0
    for k in range(FRAMES):
        spread[k // 8, COLS + k] = 1.0
    keep = np.zeros((KEPT, 384), np.float32)
    for k in range(KEPT):
        keep[k, 8 * (k // 6) + (k % 6 + 2 if k % 6 else 0)] = 1.0
    frame_pick = np.zeros((48, 384), np.float32)
    atom_pick = np.zeros((DEPTH, 384), np.float32)
    for c in range(3):
        k = 0
        for i in range(3):
            for cc in range(3):
                if cc == c:
                    frame_pick[12, c * 128 + k] = 1.0
                atom_pick[k, 8 * i + cc] = 1.0
                k += 1
        for j, i in ((0, 0), (0, 1), (0, 2), (1, 0), (1, 1), (2, 0)):
            for b in range(3):
                frame_pick[16 * j + 3 * c + b, c * 128 + k] = 1.0
                atom_pick[k, 8 * i + 3 + b] = 1.0
                k += 1
        for j in range(3):
            frame_pick[16 * j + 9 + c, c * 128 + k] = 1.0
            atom_pick[k, 6] = 1.0
            k += 1
    return jnp.asarray(np.concatenate([spread, keep, frame_pick, atom_pick]), BF16)


def dot(a, b):
    return jnp.dot(a, b, preferred_element_type=F32)


def dot_nt(a, b):
    return lax.dot_general(a, b, (((1,), (1,)), ((), ())), preferred_element_type=F32)


def pieces(x, count):
    parts = []
    for _ in range(count):
        part = x.astype(BF16).astype(F32)
        parts.append(part)
        x = x - part
    return parts


def by_type(types, values):
    total = jnp.zeros(types.shape, F32)
    for k, value in enumerate(values):
        total = jnp.where(types == k, F32(value), total)
    return total


def all_of(ref, sem):
    pltpu.make_async_copy(ref, ref, sem).wait()


def kernel(
    nx, ny, tiles,
    pf_hbm, tf_hbm, pa_hbm, ta_hbm, mask_hbm, type_hbm, swap_hbm, consts_hbm,
    out_ref,
    pf, tf, pa, ta, mask, types, swaps, consts,
    res, frames, atoms, lhs, rhs, acc_f, acc_c, packed, unpacked,
    asend, arecv, psend, precv, totals,
    in_sem, send_sem, frame_sem, atom_sem, sum_sem, part_sem, total_sem,
):
    gx, gy = lax.axis_index("gx"), lax.axis_index("gy")
    nz, nw, part = nx // 2, ny // 2, nx // 2
    z, core, w, half = lax.div(gx, 2), lax.rem(gx, 2), lax.div(gy, 2), lax.rem(gy, 2)
    near_z = [0] + [d for k in range(1, nz // 2 + 1) for d in sorted({k, nz - k})]
    near_w = [0] + [d for k in range(1, nw // 2 + 1) for d in sorted({k, nw - k})]

    def to_x(j):
        return {"gx": 2 * lax.rem(z + near_z[j // 2], nz) + lax.rem(core + j % 2, 2)}

    def from_x(j):
        return {"gx": 2 * lax.rem(z + nz - near_z[j // 2], nz) + lax.rem(core + j % 2, 2)}

    def to_y(j):
        return {"gy": 2 * lax.rem(w + near_w[j % nw], nw) + lax.rem(half + j // nw, 2)}

    def from_y(j):
        return {"gy": 2 * lax.rem(w + nw - near_w[j % nw], nw) + lax.rem(half + j // nw, 2)}

    for j in range(nx):
        atoms[j, 7:8] = jnp.zeros((1, COLS), F32)
    for j in range(ny):
        frames[j, 13:16] = jnp.zeros((3, FRAMES), F32)
    barrier = pltpu.get_barrier_semaphore()
    for j in range(1, nx):
        pl.semaphore_signal(barrier, inc=1, device_id=to_x(j), device_id_type=MESH)
    for j in range(1, ny):
        pl.semaphore_signal(barrier, inc=1, device_id=to_y(j), device_id_type=MESH)

    loads = [
        pltpu.make_async_copy(src, dst, in_sem.at[k])
        for k, (src, dst) in enumerate(
            (
                (type_hbm, types), (swap_hbm, swaps), (consts_hbm, consts), (pf_hbm, pf),
                (tf_hbm, tf), (pa_hbm, pa), (ta_hbm, ta), (mask_hbm, mask),
            )
        )
    ]
    for load in loads:
        load.start()
    res[...] = jnp.zeros_like(res)
    atoms[0] = jnp.zeros((8, COLS), F32)
    acc_f[...] = jnp.zeros_like(acc_f)
    acc_c[...] = jnp.zeros_like(acc_c)
    asend[...] = jnp.zeros_like(asend)
    psend[...] = jnp.zeros_like(psend)
    if part * ATOMS != tiles * COLS:
        packed[...] = jnp.zeros_like(packed)
    for load in loads:
        load.wait()
    spread = consts[0:RESIDUES]
    keep = consts[RESIDUES : RESIDUES + KEPT, 0:128]
    fpick = consts[RESIDUES + KEPT : RESIDUES + KEPT + 48]
    apick = consts[RESIDUES + KEPT + 48 : RESIDUES + KEPT + 48 + DEPTH, 0:24]

    kind, swap = types[...], swaps[...] == 1
    first = (kind == 3) | (kind == 13) | (kind == 18)
    third = (kind == 13) | (kind == 18)
    res[0:1, 0:RESIDUES] = by_type(kind, ATOM_COUNTS)
    res[1:2, 0:RESIDUES] = by_type(kind, CHI_COUNTS)
    res[2:3, 0:RESIDUES] = jnp.where(first & swap, F32(1), F32(0))
    res[3:4, 0:RESIDUES] = jnp.where((kind == 6) & swap, F32(1), F32(0))
    res[4:5, 0:RESIDUES] = jnp.where(third & swap, F32(1), F32(0))
    of_both = dot(res[:, 0:RESIDUES].astype(BF16), spread)
    of_atom, of_frame = of_both[:, :COLS], of_both[:, COLS:]

    lane = lax.broadcasted_iota(jnp.int32, (1, COLS), 1)
    slot = lane - 14 * ((lane * 4682) >> 16)
    swap_a, swap_b, swap_c = (of_atom[k : k + 1] > 0.5 for k in (2, 3, 4))
    upper = ((slot == 6) & swap_a) | ((slot == 7) & swap_b) | ((slot == 8) & swap_c)
    lower = ((slot == 7) & swap_a) | ((slot == 8) & swap_b) | ((slot == 9) & swap_c)
    atoms[0, 0:3, 0:ATOMS] = pa[...]
    atoms[0, 3:6, 0:ATOMS] = ta[...]
    atoms[0, 6:7, 0:ATOMS] = mask[...].astype(F32)
    raw = atoms[0]
    row = lax.broadcasted_iota(jnp.int32, (8, COLS), 0)
    renamed = jnp.where(
        upper & (row >= 3), pltpu.roll(raw, COLS - 1, 1),
        jnp.where(lower & (row >= 3), pltpu.roll(raw, 1, 1), raw),
    )
    weight = jnp.where(slot.astype(F32) < of_atom[0:1], renamed[6:7], F32(0))
    atoms[0] = renamed * jnp.where(row < 3, F32(0.1), F32(1.0)) * weight

    group = lax.broadcasted_iota(jnp.int32, (1, FRAMES), 1) & 7
    exists = jnp.where(
        (group == 0) | (group == 3) | ((group >= 4) & ((group - 3).astype(F32) <= of_frame[1:2])),
        F32(1), F32(0),
    )
    flips = ((group == 5) & (of_frame[2:3] > 0.5)) | ((group == 6) & (of_frame[3:4] > 0.5))
    sign = jnp.where(flips, F32(-1), F32(1))
    rot_p = [pf[k : k + 1] for k in range(12)]
    rot_t = [tf[k : k + 1] * sign if k % 3 and k < 9 else tf[k : k + 1] for k in range(12)]
    scale = -0.1 * exists
    for a in range(3):
        moved = rot_p[9 + a] * scale
        for b in range(3):
            turn = scale * (
                rot_p[3 * a] * rot_t[3 * b]
                + rot_p[3 * a + 1] * rot_t[3 * b + 1]
                + rot_p[3 * a + 2] * rot_t[3 * b + 2]
            )
            frames[0, 3 * a + b : 3 * a + b + 1] = turn
            moved = moved - turn * rot_t[9 + b]
        frames[0, 9 + a : 10 + a] = moved
    frames[0, 12:13] = exists

    pl.semaphore_wait(barrier, nx - 1 + ny - 1)

    if nx == 16:
        atom_tiers, tile_tiers = (0, 6, 8, 14, 16), (0, 5, 7, 12, 14)
    else:
        atom_tiers, tile_tiers = (0, part, part, nx, nx), (0, tiles, tiles, 2 * tiles, 2 * tiles)
    frame_tiers = (0, 3, 5, 7, 8) if ny == 8 else (0, 1, nw, ny, ny)
    tier_of = [k for k in range(4) for _ in range(atom_tiers[k], atom_tiers[k + 1])]

    def send_atoms(j):
        pltpu.make_async_remote_copy(
            atoms.at[0, 0:7], atoms.at[j, 0:7], send_sem.at[1], atom_sem.at[tier_of[j]],
            to_x(j), MESH,
        ).start()

    for j in range(1, part):
        send_atoms(j)
    for j in range(1, ny):
        pltpu.make_async_remote_copy(
            frames.at[0, 0:13], frames.at[j, 0:13], send_sem.at[0], frame_sem.at[j],
            to_y(j), MESH,
        ).start()
    for j in range(part, nx):
        send_atoms(j)

    chunks = KEPT // FB

    def frame_side(s):
        split = jnp.concatenate(pieces(frames[s], 3), axis=0).astype(BF16)
        turned = dot_nt(keep, split).astype(BF16)
        side = dot(turned, fpick).astype(BF16)
        for q in range(chunks):
            for c in range(3):
                lhs[s * chunks + q, c * FB : (c + 1) * FB] = side[
                    q * FB : (q + 1) * FB, c * 128 : c * 128 + DEPTH
                ]

    def atom_side(tier):
        low, high = tile_tiers[tier : tier + 2]
        for j in range(*atom_tiers[tier : tier + 2]):
            k = j % part * ATOMS
            packed[j // part, :, k : k + ATOMS] = atoms[j, :, 0:ATOMS]
        group, first = low // tiles, low % tiles
        lanes = packed[group, :, first * COLS : (first + high - low) * COLS]
        split = jnp.concatenate(pieces(lanes, 3), axis=0).astype(BF16)
        side = dot(apick, split).astype(BF16)
        for t in range(high - low):
            rhs[low + t] = side[:, t * COLS : (t + 1) * COLS]

    def pairs_of(blocks):
        for low, high, first, last in blocks:
            sums = [acc_c[t] for t in range(first, last)]
            for q in range(low * chunks, high * chunks):
                total = jnp.zeros((FB, 128), F32)
                for k in range(last - first):
                    e = dot(lhs[q], rhs[first + k])
                    e0, e1, e2 = e[:FB], e[FB : 2 * FB], e[2 * FB :]
                    y = jnp.minimum((e0 * e0 + e1 * e1) + (e2 * e2 + EPS), 1.0)
                    clamped = y * lax.rsqrt(y)
                    side = clamped[:, :128] + clamped[:, 128:]
                    total = side if k == 0 else total + side
                    sums[k] = sums[k] + clamped.reshape(FB // 8, 8, COLS).sum(axis=0)
                acc_f[q * FB : (q + 1) * FB] += total
            for k, value in enumerate(sums):
                acc_c[first + k] = value

    def column_rows():
        total = jnp.zeros((1, COLS), F32)
        for t in range(2 * tiles):
            row = acc_c[t].sum(axis=0, keepdims=True)
            k = t % tiles * COLS
            unpacked[t // tiles : t // tiles + 1, k : k + COLS] = row
            total = total + row
        return total

    def send_sums(group, frame_flags):
        for k in range(part):
            j = group * part + k
            asend[j, :, 0:ATOMS] = unpacked[group : group + 1, k * ATOMS : (k + 1) * ATOMS]
            asend[j, :, ATOMS : ATOMS + 1] = frame_flags
        for j in range(max(1, group * part), (group + 1) * part):
            pltpu.make_async_remote_copy(
                asend.at[j], arecv.at[j], send_sem.at[2], sum_sem.at[0], from_x(j), MESH
            ).start()

    held = []
    for tier in range(4):
        first, last = tile_tiers[tier : tier + 2]
        low, high = frame_tiers[tier : tier + 2]
        slots = atom_tiers[tier : tier + 2]
        if tier == 0:
            frame_side(0)
        if max(1, slots[0]) < slots[1]:
            all_of(atoms.at[max(1, slots[0]) : slots[1], 0:7], atom_sem.at[tier])
        for s in range(max(1, low), high):
            all_of(frames.at[s, 0:13], frame_sem.at[s])
        for s in range(max(1, low), high):
            frame_side(s)
        if first < last:
            atom_side(tier)
        pairs_of(held)
        blocks = []
        if first < last:
            blocks.append((0, low, first, last))
        for s in range(low, high):
            for group in range(2):
                bounds = max(0, group * tiles), min(last, (group + 1) * tiles)
                if bounds[0] < bounds[1]:
                    blocks.append((s, s + 1, *bounds))
        blocks = [b for b in blocks if b[0] < b[1]]
        hold = 1 if tier < 3 else 0
        held = blocks[len(blocks) - hold :]
        pairs_of(blocks[: len(blocks) - hold])
    flags = frames[0, 12:13]
    for s in range(1, ny):
        flags = flags + frames[s, 12:13]
    flags = jnp.sum(flags, axis=1, keepdims=True)
    running = column_rows()

    def hops(jx, jy):
        dz, dw = near_z[jx // 2], near_w[jy % nw]
        return min(dz, nz - dz) + min(dw, nw - dw) + 2 * (jy // nw)

    others = sorted(
        ((jx, jy) for jx in range(nx) for jy in range(ny) if jx or jy), key=lambda j: -hops(*j)
    )

    def send_total(jx, jy):
        k = jx * ny + jy
        pltpu.make_async_remote_copy(
            totals.at[0:1], totals.at[k : k + 1], send_sem.at[3], total_sem.at[0],
            {**to_x(jx), **to_y(jy)}, MESH,
        ).start()

    totals[0:1] = running[:, :128] + running[:, 128:]
    first_sent = len(others) // 2
    for j in others[:first_sent]:
        send_total(*j)
    send_sums(0, flags)
    send_sums(1, flags)

    ones = jnp.ones((8, 128), BF16)
    weights = jnp.zeros((1, COLS), F32)
    for j in range(nx):
        weights = weights + atoms[j, 6:7]
    weights = jnp.sum(weights, axis=1, keepdims=True)
    for s in range(ny):
        partial = jnp.zeros((8, KEPT), F32)
        for piece in pieces(acc_f[s * KEPT : (s + 1) * KEPT], 3):
            partial = partial + dot_nt(ones, piece.astype(BF16))
        psend[s, :, 0:KEPT] = partial[0:1]
        psend[s, :, KEPT : KEPT + 1] = weights
    for s in range(1, ny):
        pltpu.make_async_remote_copy(
            psend.at[s], precv.at[s], send_sem.at[4], part_sem.at[0], from_y(s), MESH
        ).start()
    for j in others[first_sent:]:
        send_total(*j)

    columns = F32(2 * tiles * ny * COLS)
    rows = F32(nx * ny * KEPT)
    all_of(precv.at[1:ny], part_sem.at[0])
    mine = psend[0]
    for s in range(1, ny):
        mine = mine + precv[s]
    atom_count = mine[:, KEPT : KEPT + 1]
    least_y = jnp.zeros((1, 128), F32) * mine + EPS
    least = least_y * lax.rsqrt(least_y)
    own_sum = jnp.zeros((8, FRAMES), F32)
    for piece in pieces(jnp.broadcast_to(mine[:, :KEPT], (8, KEPT)), 3):
        own_sum = own_sum + dot(piece.astype(BF16), keep)
    out_ref[0:1, 0:FRAMES] = (
        frames[0, 12:13] * (own_sum[0:1] - (columns - atom_count) * least) / atom_count
    )
    all_of(arecv.at[1:nx], sum_sem.at[0])
    asum = asend[0]
    for j in range(1, nx):
        asum = asum + arecv[j]
    frame_count = asum[:, ATOMS : ATOMS + 1]
    wide = jnp.concatenate([least, least], axis=1)
    out_ref[1:2, :] = atoms[0, 6:7] * (asum - (rows - frame_count) * wide) / frame_count
    pairs = frame_count * atom_count

    all_of(totals.at[1 : nx * ny], total_sem.at[0])
    numerator = jnp.sum(
        jnp.sum(totals[...], axis=0, keepdims=True), axis=1, keepdims=True
    )
    out_ref[2:3, 0:128] = (numerator - least * (rows * columns - pairs)) / pairs

    all_of(frames.at[1:ny, 0:13], send_sem.at[0])
    all_of(atoms.at[1:nx, 0:7], send_sem.at[1])
    all_of(arecv.at[1:nx], send_sem.at[2])
    all_of(totals.at[1 : nx * ny], send_sem.at[3])
    all_of(precv.at[1:ny], send_sem.at[4])


def shards(nx, ny, pred_frames, true_frames, pred_atoms, true_atoms, atom_mask, residue_types, swap_flags):
    dma = pltpu.SemaphoreType.DMA
    blocks = ny * KEPT // FB
    tiles = -(-nx // 2 * ATOMS // COLS)
    ins = (
        pred_frames, true_frames, pred_atoms, true_atoms, atom_mask.reshape(1, ATOMS),
        residue_types.reshape(1, RESIDUES), swap_flags.reshape(1, RESIDUES), tables(),
    )
    packed = pl.pallas_call(
        functools.partial(kernel, nx, ny, tiles),
        out_shape=pltpu.VMEM((8, COLS), F32),
        in_specs=[pl.BlockSpec(memory_space=pl.ANY)] * len(ins),
        out_specs=pl.BlockSpec(memory_space=pltpu.VMEM),
        scratch_shapes=[pltpu.VMEM(a.shape, a.dtype) for a in ins]
        + [
            pltpu.VMEM((8, 128), F32),
            pltpu.VMEM((ny, 16, FRAMES), F32),
            pltpu.VMEM((nx, 8, COLS), F32),
            pltpu.VMEM((blocks, 3 * FB, DEPTH), BF16),
            pltpu.VMEM((2 * tiles, DEPTH, COLS), BF16),
            pltpu.VMEM((ny * KEPT, 128), F32),
            pltpu.VMEM((2 * tiles, 8, COLS), F32),
            pltpu.VMEM((2, 8, tiles * COLS), F32),
            pltpu.VMEM((8, tiles * COLS), F32),
            pltpu.VMEM((nx, 1, COLS), F32),
            pltpu.VMEM((nx, 1, COLS), F32),
            pltpu.VMEM((ny, 1, 128), F32),
            pltpu.VMEM((ny, 1, 128), F32),
            pltpu.VMEM((nx * ny, 128), F32),
            dma((len(ins),)), dma((5,)), dma((ny,)), dma((4,)), dma((1,)), dma((1,)), dma((1,)),
        ],
        compiler_params=pltpu.CompilerParams(collective_id=0, has_side_effects=True),
        name="fape",
    )(*ins)
    return packed[0, :FRAMES], packed[1, :ATOMS], packed[2, :1]


def solution(mesh):
    whole = ("sa", "gx", "gy")
    wide, flat = P(None, whole), P(whole)
    return jax.shard_map(
        functools.partial(shards, mesh.shape["gx"], mesh.shape["gy"]),
        mesh=mesh,
        in_specs=(wide, wide, wide, wide, flat, flat, flat),
        out_specs=(flat, flat, P("sa")),
        check_vma=False,
    )
```

```python
import functools

import jax
import jax.numpy as jnp
import numpy as np
from jax import lax
from jax.experimental import pallas as pl
from jax.experimental.pallas import tpu as pltpu
from jax.sharding import PartitionSpec as P

F32 = jnp.float32
BF16 = jnp.bfloat16
MESH = pl.DeviceIdType.MESH

RESIDUES = 16
FRAMES = 8 * RESIDUES
ATOMS = 14 * RESIDUES
KEPT = 6 * RESIDUES
COLS = 256
FB = 32
DEPTH = 32
EPS = 1e-6
ATOM_COUNTS = (5, 11, 8, 8, 6, 9, 9, 4, 10, 8, 8, 9, 8, 11, 7, 6, 7, 14, 12, 7)
CHI_COUNTS = (0, 4, 2, 2, 1, 3, 3, 0, 2, 2, 2, 4, 3, 2, 2, 1, 1, 2, 2, 1)


def tables():
    spread = np.zeros((RESIDUES, 384), np.float32)
    for k in range(ATOMS):
        spread[k // 14, k] = 1.0
    for k in range(FRAMES):
        spread[k // 8, COLS + k] = 1.0
    keep = np.zeros((KEPT, 384), np.float32)
    for k in range(KEPT):
        keep[k, 8 * (k // 6) + (k % 6 + 2 if k % 6 else 0)] = 1.0
    frame_pick = np.zeros((48, 384), np.float32)
    atom_pick = np.zeros((DEPTH, 384), np.float32)
    for c in range(3):
        k = 0
        for i in range(3):
            for cc in range(3):
                if cc == c:
                    frame_pick[12, c * 128 + k] = 1.0
                atom_pick[k, 8 * i + cc] = 1.0
                k += 1
        for j, i in ((0, 0), (0, 1), (0, 2), (1, 0), (1, 1), (2, 0)):
            for b in range(3):
                frame_pick[16 * j + 3 * c + b, c * 128 + k] = 1.0
                atom_pick[k, 8 * i + 3 + b] = 1.0
                k += 1
        for j in range(3):
            frame_pick[16 * j + 9 + c, c * 128 + k] = 1.0
            atom_pick[k, 6] = 1.0
            k += 1
    return jnp.asarray(np.concatenate([spread, keep, frame_pick, atom_pick]), BF16)


def dot(a, b):
    return jnp.dot(a, b, preferred_element_type=F32)


def dot_nt(a, b):
    return lax.dot_general(a, b, (((1,), (1,)), ((), ())), preferred_element_type=F32)


def pieces(x, count):
    parts = []
    for _ in range(count):
        part = x.astype(BF16).astype(F32)
        parts.append(part)
        x = x - part
    return parts


def by_type(types, values):
    total = jnp.zeros(types.shape, F32)
    for k, value in enumerate(values):
        total = jnp.where(types == k, F32(value), total)
    return total


def all_of(ref, sem):
    pltpu.make_async_copy(ref, ref, sem).wait()


def kernel(
    nx, ny, tiles,
    pf_hbm, tf_hbm, pa_hbm, ta_hbm, mask_hbm, type_hbm, swap_hbm, consts_hbm,
    out_ref,
    pf, tf, pa, ta, mask, types, swaps, consts,
    res, frames, atoms, lhs, rhs, acc_f, acc_c, packed, unpacked,
    asend, arecv, psend, precv, totals,
    in_sem, send_sem, frame_sem, atom_sem, sum_sem, part_sem, total_sem,
):
    gx, gy = lax.axis_index("gx"), lax.axis_index("gy")
    nz, nw, part = nx // 2, ny // 2, nx // 2
    z, core, w, half = lax.div(gx, 2), lax.rem(gx, 2), lax.div(gy, 2), lax.rem(gy, 2)
    near_z = [0] + [d for k in range(1, nz // 2 + 1) for d in sorted({k, nz - k})]
    near_w = [0] + [d for k in range(1, nw // 2 + 1) for d in sorted({k, nw - k})]

    ahead = [2 * lax.rem(z + d, nz) for d in near_z]
    behind = [2 * lax.rem(z + nz - d, nz) for d in near_z]
    ahead_w = [2 * lax.rem(w + d, nw) for d in near_w]
    behind_w = [2 * lax.rem(w + nw - d, nw) for d in near_w]
    cores, halves = (core, 1 - core), (half, 1 - half)

    def to_x(j):
        return {"gx": ahead[j // 2] + cores[j % 2]}

    def from_x(j):
        return {"gx": behind[j // 2] + cores[j % 2]}

    def to_y(j):
        return {"gy": ahead_w[j % nw] + halves[j // nw]}

    def from_y(j):
        return {"gy": behind_w[j % nw] + halves[j // nw]}

    loads = [
        pltpu.make_async_copy(src, dst, in_sem.at[k])
        for k, (src, dst) in enumerate(
            (
                (type_hbm, types), (swap_hbm, swaps), (consts_hbm, consts), (pf_hbm, pf),
                (tf_hbm, tf), (pa_hbm, pa), (ta_hbm, ta), (mask_hbm, mask),
            )
        )
    ]
    for load in loads:
        load.start()
    for j in range(nx):
        atoms[j, 7:8] = jnp.zeros((1, COLS), F32)
    for j in range(ny):
        frames[j, 13:16] = jnp.zeros((3, FRAMES), F32)
    barrier = pltpu.get_barrier_semaphore()
    for j in range(1, nx):
        pl.semaphore_signal(barrier, inc=1, device_id=to_x(j), device_id_type=MESH)
    for j in range(1, ny):
        pl.semaphore_signal(barrier, inc=1, device_id=to_y(j), device_id_type=MESH)

    res[...] = jnp.zeros_like(res)
    atoms[0] = jnp.zeros((8, COLS), F32)
    acc_f[...] = jnp.zeros_like(acc_f)
    acc_c[...] = jnp.zeros_like(acc_c)
    asend[...] = jnp.zeros_like(asend)
    psend[...] = jnp.zeros_like(psend)
    if part * ATOMS != tiles * COLS:
        packed[...] = jnp.zeros_like(packed)
    for load in loads:
        load.wait()
    spread = consts[0:RESIDUES]
    keep = consts[RESIDUES : RESIDUES + KEPT, 0:128]
    fpick = consts[RESIDUES + KEPT : RESIDUES + KEPT + 48]
    apick = consts[RESIDUES + KEPT + 48 : RESIDUES + KEPT + 48 + DEPTH, 0:24]

    kind, swap = types[...], swaps[...] == 1
    first = (kind == 3) | (kind == 13) | (kind == 18)
    third = (kind == 13) | (kind == 18)
    res[0:1, 0:RESIDUES] = by_type(kind, ATOM_COUNTS)
    res[1:2, 0:RESIDUES] = by_type(kind, CHI_COUNTS)
    res[2:3, 0:RESIDUES] = jnp.where(first & swap, F32(1), F32(0))
    res[3:4, 0:RESIDUES] = jnp.where((kind == 6) & swap, F32(1), F32(0))
    res[4:5, 0:RESIDUES] = jnp.where(third & swap, F32(1), F32(0))
    of_both = dot(res[:, 0:RESIDUES].astype(BF16), spread)
    of_atom, of_frame = of_both[:, :COLS], of_both[:, COLS:]

    lane = lax.broadcasted_iota(jnp.int32, (1, COLS), 1)
    slot = lane - 14 * ((lane * 4682) >> 16)
    swap_a, swap_b, swap_c = (of_atom[k : k + 1] > 0.5 for k in (2, 3, 4))
    upper = ((slot == 6) & swap_a) | ((slot == 7) & swap_b) | ((slot == 8) & swap_c)
    lower = ((slot == 7) & swap_a) | ((slot == 8) & swap_b) | ((slot == 9) & swap_c)
    atoms[0, 0:3, 0:ATOMS] = pa[...]
    atoms[0, 3:6, 0:ATOMS] = ta[...]
    atoms[0, 6:7, 0:ATOMS] = mask[...].astype(F32)
    raw = atoms[0]
    row = lax.broadcasted_iota(jnp.int32, (8, COLS), 0)
    renamed = jnp.where(
        upper & (row >= 3), pltpu.roll(raw, COLS - 1, 1),
        jnp.where(lower & (row >= 3), pltpu.roll(raw, 1, 1), raw),
    )
    weight = jnp.where(slot.astype(F32) < of_atom[0:1], renamed[6:7], F32(0))
    atoms[0] = renamed * jnp.where(row < 3, F32(0.1), F32(1.0)) * weight

    group = lax.broadcasted_iota(jnp.int32, (1, FRAMES), 1) & 7
    exists = jnp.where(
        (group == 0) | (group == 3) | ((group >= 4) & ((group - 3).astype(F32) <= of_frame[1:2])),
        F32(1), F32(0),
    )
    flips = ((group == 5) & (of_frame[2:3] > 0.5)) | ((group == 6) & (of_frame[3:4] > 0.5))
    sign = jnp.where(flips, F32(-1), F32(1))
    rot_p = [pf[k : k + 1] for k in range(12)]
    rot_t = [tf[k : k + 1] * sign if k % 3 and k < 9 else tf[k : k + 1] for k in range(12)]
    scale = -0.1 * exists
    for a in range(3):
        moved = rot_p[9 + a] * scale
        for b in range(3):
            turn = scale * (
                rot_p[3 * a] * rot_t[3 * b]
                + rot_p[3 * a + 1] * rot_t[3 * b + 1]
                + rot_p[3 * a + 2] * rot_t[3 * b + 2]
            )
            frames[0, 3 * a + b : 3 * a + b + 1] = turn
            moved = moved - turn * rot_t[9 + b]
        frames[0, 9 + a : 10 + a] = moved
    frames[0, 12:13] = exists

    pl.semaphore_wait(barrier, nx - 1 + ny - 1)

    if nx == 16:
        atom_tiers, tile_tiers = (0, 6, 8, 14, 16), (0, 5, 7, 12, 14)
    else:
        atom_tiers, tile_tiers = (0, part, part, nx, nx), (0, tiles, tiles, 2 * tiles, 2 * tiles)
    frame_tiers = (0, 3, 5, 7, 8) if ny == 8 else (0, 1, nw, ny, ny)
    tier_of = [k for k in range(4) for _ in range(atom_tiers[k], atom_tiers[k + 1])]

    def send_atoms(j):
        pltpu.make_async_remote_copy(
            atoms.at[0, 0:7], atoms.at[j, 0:7], send_sem.at[1], atom_sem.at[tier_of[j]],
            to_x(j), MESH,
        ).start()

    for j in range(1, part):
        send_atoms(j)
    for j in range(1, ny):
        pltpu.make_async_remote_copy(
            frames.at[0, 0:13], frames.at[j, 0:13], send_sem.at[0], frame_sem.at[j],
            to_y(j), MESH,
        ).start()
    for j in range(part, nx):
        send_atoms(j)

    chunks = KEPT // FB

    def frame_side(s):
        split = jnp.concatenate(pieces(frames[s], 3), axis=0).astype(BF16)
        turned = dot_nt(keep, split).astype(BF16)
        side = dot(turned, fpick).astype(BF16)
        for q in range(chunks):
            for c in range(3):
                lhs[s * chunks + q, c * FB : (c + 1) * FB] = side[
                    q * FB : (q + 1) * FB, c * 128 : c * 128 + DEPTH
                ]

    def atom_side(tier):
        low, high = tile_tiers[tier : tier + 2]
        for j in range(*atom_tiers[tier : tier + 2]):
            k = j % part * ATOMS
            packed[j // part, :, k : k + ATOMS] = atoms[j, :, 0:ATOMS]
        group, first = low // tiles, low % tiles
        lanes = packed[group, :, first * COLS : (first + high - low) * COLS]
        split = jnp.concatenate(pieces(lanes, 3), axis=0).astype(BF16)
        side = dot(apick, split).astype(BF16)
        for t in range(high - low):
            rhs[low + t] = side[:, t * COLS : (t + 1) * COLS]

    def pairs_of(blocks):
        for low, high, first, last in blocks:
            sums = [acc_c[t] for t in range(first, last)]
            for q in range(low * chunks, high * chunks):
                total = jnp.zeros((FB, 128), F32)
                for k in range(last - first):
                    e = dot(lhs[q], rhs[first + k])
                    e0, e1, e2 = e[:FB], e[FB : 2 * FB], e[2 * FB :]
                    y = jnp.minimum((e0 * e0 + e1 * e1) + (e2 * e2 + EPS), 1.0)
                    clamped = y * lax.rsqrt(y)
                    side = clamped[:, :128] + clamped[:, 128:]
                    total = side if k == 0 else total + side
                    sums[k] = sums[k] + clamped.reshape(FB // 8, 8, COLS).sum(axis=0)
                acc_f[q * FB : (q + 1) * FB] += total
            for k, value in enumerate(sums):
                acc_c[first + k] = value

    def column_rows():
        total = jnp.zeros((1, COLS), F32)
        for t in range(2 * tiles):
            row = acc_c[t].sum(axis=0, keepdims=True)
            k = t % tiles * COLS
            unpacked[t // tiles : t // tiles + 1, k : k + COLS] = row
            total = total + row
        return total

    def send_sums(group, frame_flags):
        for k in range(part):
            j = group * part + k
            asend[j, :, 0:ATOMS] = unpacked[group : group + 1, k * ATOMS : (k + 1) * ATOMS]
            asend[j, :, ATOMS : ATOMS + 1] = frame_flags
        for j in range(max(1, group * part), (group + 1) * part):
            pltpu.make_async_remote_copy(
                asend.at[j], arecv.at[j], send_sem.at[2], sum_sem.at[0], from_x(j), MESH
            ).start()

    held = []
    for tier in range(4):
        first, last = tile_tiers[tier : tier + 2]
        low, high = frame_tiers[tier : tier + 2]
        slots = atom_tiers[tier : tier + 2]
        if tier == 0:
            frame_side(0)
        if max(1, slots[0]) < slots[1]:
            all_of(atoms.at[max(1, slots[0]) : slots[1], 0:7], atom_sem.at[tier])
        for s in range(max(1, low), high):
            all_of(frames.at[s, 0:13], frame_sem.at[s])
        for s in range(max(1, low), high):
            frame_side(s)
        if first < last:
            atom_side(tier)
        pairs_of(held)
        blocks = []
        if first < last:
            blocks.append((0, low, first, last))
        for s in range(low, high):
            for group in range(2):
                bounds = max(0, group * tiles), min(last, (group + 1) * tiles)
                if bounds[0] < bounds[1]:
                    blocks.append((s, s + 1, *bounds))
        blocks = [b for b in blocks if b[0] < b[1]]
        hold = 1 if tier < 3 else 0
        held = blocks[len(blocks) - hold :]
        pairs_of(blocks[: len(blocks) - hold])
    flags = frames[0, 12:13]
    for s in range(1, ny):
        flags = flags + frames[s, 12:13]
    flags = jnp.sum(flags, axis=1, keepdims=True)
    running = column_rows()

    def hops(jx, jy):
        dz, dw = near_z[jx // 2], near_w[jy % nw]
        return min(dz, nz - dz) + min(dw, nw - dw) + 2 * (jy // nw)

    others = sorted(
        ((jx, jy) for jx in range(nx) for jy in range(ny) if jx or jy), key=lambda j: -hops(*j)
    )

    def send_total(jx, jy):
        k = jx * ny + jy
        pltpu.make_async_remote_copy(
            totals.at[0:1], totals.at[k : k + 1], send_sem.at[3], total_sem.at[0],
            {**to_x(jx), **to_y(jy)}, MESH,
        ).start()

    totals[0:1] = running[:, :128] + running[:, 128:]
    first_sent = len(others) // 2
    for j in others[:first_sent]:
        send_total(*j)
    send_sums(0, flags)
    send_sums(1, flags)

    ones = jnp.ones((8, 128), BF16)
    weights = jnp.zeros((1, COLS), F32)
    for j in range(nx):
        weights = weights + atoms[j, 6:7]
    weights = jnp.sum(weights, axis=1, keepdims=True)
    for s in range(ny):
        partial = jnp.zeros((8, KEPT), F32)
        for piece in pieces(acc_f[s * KEPT : (s + 1) * KEPT], 3):
            partial = partial + dot_nt(ones, piece.astype(BF16))
        psend[s, :, 0:KEPT] = partial[0:1]
        psend[s, :, KEPT : KEPT + 1] = weights
    for s in range(1, ny):
        pltpu.make_async_remote_copy(
            psend.at[s], precv.at[s], send_sem.at[4], part_sem.at[0], from_y(s), MESH
        ).start()
    for j in others[first_sent:]:
        send_total(*j)

    columns = F32(2 * tiles * ny * COLS)
    rows = F32(nx * ny * KEPT)
    all_of(precv.at[1:ny], part_sem.at[0])
    mine = psend[0]
    for s in range(1, ny):
        mine = mine + precv[s]
    atom_count = mine[:, KEPT : KEPT + 1]
    least_y = jnp.zeros((1, 128), F32) * mine + EPS
    least = least_y * lax.rsqrt(least_y)
    own_sum = jnp.zeros((8, FRAMES), F32)
    for piece in pieces(jnp.broadcast_to(mine[:, :KEPT], (8, KEPT)), 3):
        own_sum = own_sum + dot(piece.astype(BF16), keep)
    out_ref[0:1, 0:FRAMES] = (
        frames[0, 12:13] * (own_sum[0:1] - (columns - atom_count) * least) / atom_count
    )
    all_of(arecv.at[1:nx], sum_sem.at[0])
    asum = asend[0]
    for j in range(1, nx):
        asum = asum + arecv[j]
    frame_count = asum[:, ATOMS : ATOMS + 1]
    wide = jnp.concatenate([least, least], axis=1)
    out_ref[1:2, :] = atoms[0, 6:7] * (asum - (rows - frame_count) * wide) / frame_count
    pairs = frame_count * atom_count

    all_of(totals.at[1 : nx * ny], total_sem.at[0])
    numerator = jnp.sum(
        jnp.sum(totals[...], axis=0, keepdims=True), axis=1, keepdims=True
    )
    out_ref[2:3, 0:128] = (numerator - least * (rows * columns - pairs)) / pairs

    all_of(frames.at[1:ny, 0:13], send_sem.at[0])
    all_of(atoms.at[1:nx, 0:7], send_sem.at[1])
    all_of(arecv.at[1:nx], send_sem.at[2])
    all_of(totals.at[1 : nx * ny], send_sem.at[3])
    all_of(precv.at[1:ny], send_sem.at[4])


def shards(nx, ny, pred_frames, true_frames, pred_atoms, true_atoms, atom_mask, residue_types, swap_flags):
    dma = pltpu.SemaphoreType.DMA
    blocks = ny * KEPT // FB
    tiles = -(-nx // 2 * ATOMS // COLS)
    ins = (
        pred_frames, true_frames, pred_atoms, true_atoms, atom_mask.reshape(1, ATOMS),
        residue_types.reshape(1, RESIDUES), swap_flags.reshape(1, RESIDUES), tables(),
    )
    packed = pl.pallas_call(
        functools.partial(kernel, nx, ny, tiles),
        out_shape=pltpu.VMEM((8, COLS), F32),
        in_specs=[pl.BlockSpec(memory_space=pl.ANY)] * len(ins),
        out_specs=pl.BlockSpec(memory_space=pltpu.VMEM),
        scratch_shapes=[pltpu.VMEM(a.shape, a.dtype) for a in ins]
        + [
            pltpu.VMEM((8, 128), F32),
            pltpu.VMEM((ny, 16, FRAMES), F32),
            pltpu.VMEM((nx, 8, COLS), F32),
            pltpu.VMEM((blocks, 3 * FB, DEPTH), BF16),
            pltpu.VMEM((2 * tiles, DEPTH, COLS), BF16),
            pltpu.VMEM((ny * KEPT, 128), F32),
            pltpu.VMEM((2 * tiles, 8, COLS), F32),
            pltpu.VMEM((2, 8, tiles * COLS), F32),
            pltpu.VMEM((8, tiles * COLS), F32),
            pltpu.VMEM((nx, 1, COLS), F32),
            pltpu.VMEM((nx, 1, COLS), F32),
            pltpu.VMEM((ny, 1, 128), F32),
            pltpu.VMEM((ny, 1, 128), F32),
            pltpu.VMEM((nx * ny, 128), F32),
            dma((len(ins),)), dma((5,)), dma((ny,)), dma((4,)), dma((1,)), dma((1,)), dma((1,)),
        ],
        compiler_params=pltpu.CompilerParams(collective_id=0, has_side_effects=True),
        name="fape",
    )(*ins)
    return packed[0, :FRAMES], packed[1, :ATOMS], packed[2, :1]


def solution(mesh):
    whole = ("sa", "gx", "gy")
    wide, flat = P(None, whole), P(whole)
    return jax.shard_map(
        functools.partial(shards, mesh.shape["gx"], mesh.shape["gy"]),
        mesh=mesh,
        in_specs=(wide, wide, wide, wide, flat, flat, flat),
        out_specs=(flat, flat, P("sa")),
        check_vma=False,
    )
```
